512 devices in a mesh: grp: 64 (over y, z), span: 8 (over x, core).
Axes of the slice: x: 4, y: 8, z: 8, core: 2. Of those that a mesh axis runs over, the one named last changes fastest.
Arguments:
- slopes: bfloat16 [65536, 1024], P(('grp', 'span')), may hold values from -6 to 6
- reconstructor: bfloat16 [1024, 512], P('span'), may hold values from -0.1875 to 0.1875
- interaction: bfloat16 [512, 1024], P(None, 'span'), may hold values from -0.25 to 0.25
- frame_valid: int32 [512], P(('grp', 'span')), may hold values 0 or 1
- open_rate: float32 [512], replicated, may hold values from 3.8146973e-07 to 0.021, as said below
- closed_rate: float32 [512], replicated, may hold values from 3.8146973e-06 to 0.034
Outputs:
- smoothed: bfloat16 [65536, 512], P(('grp', 'span'))
- residual: bfloat16 [65536, 1024], P(('grp', 'span'))
The draws below stay inside these ranges and needn't reach their ends.
Inputs may be any that keep to these rules, and one draw needn't show every extreme that they name: For every mode, open_rate is below closed_rate.
All inputs are finite; a program needn't handle non-finite values. No bound on the sum of `frame_valid` on one device may be relied on, other than what follows from the above.
Results may differ from the reference program's by a relative error of at most 0.02.
Values may be sent and summed in bfloat16 or wider, within the bound.
A program may use at most 64 MiB of HBM per device.

```python
import jax
import jax.numpy as jnp
from jax import lax

STATE_MODES = 512
SENSOR_SLOPES = 1024
BLOCK_FRAMES = 128
T_DEV = 128
TOTAL_FRAMES = 65536
NBLK = 512


def mode_rates(key):
    base = jax.random.fold_in(key, 7)
    first, second, third, fourth = jax.random.split(base, 4)
    share = 0.5
    slow = jax.random.uniform(first, (STATE_MODES,)) < share
    spread = jax.random.uniform(second, (STATE_MODES,))
    slow_rate = jnp.exp(jnp.log(0.25 / TOTAL_FRAMES) + spread * jnp.log(8.0))
    other = jax.random.uniform(third, (STATE_MODES,))
    low_end = 0.05 / T_DEV
    high_end = 1.0 / 30.0
    other_rate = jnp.exp(jnp.log(low_end) + other * jnp.log(high_end / low_end))
    closed = jnp.where(slow, slow_rate, other_rate)
    ratio = jax.random.uniform(fourth, (STATE_MODES,), minval=0.1, maxval=0.6)
    return (closed * ratio, closed)


def draw_open_rate(key, part):
    return mode_rates(key)[0].astype(jnp.float32)


def draw_closed_rate(key, part):
    return mode_rates(key)[1].astype(jnp.float32)


def with_ends(array, stream_key, low, largest):
    shape = array.shape
    index_at = [jax.random.randint(jax.random.fold_in(stream_key, axis), (), 0, shape[axis]) for axis in range(len(shape))]
    array = array.at[tuple(index_at)].set(low)
    longest = shape.index(max(shape))
    index_at[longest] = (index_at[longest] + 1) % shape[longest]
    return array.at[tuple(index_at)].set(largest)


def level_of(stream_key, dims, shards, smallest, high):
    loudness = 1.0
    for axis_at, parts in shards:
        draws = jax.random.uniform(jax.random.fold_in(jax.random.fold_in(stream_key, 6), axis_at), (parts,), jnp.float32, smallest / len(shards), high / len(shards))
        loudness = loudness * jnp.repeat(jnp.exp(draws), dims[axis_at] // parts).reshape((-1,) + (1,) * (len(dims) - 1 - axis_at))
    return loudness


def bell_draw(key, extent, scale, bound, shards=(), dtype=jnp.bfloat16):
    values = scale * jax.random.normal(key, extent, jnp.float32)
    if shards:
        values = values * level_of(key, extent, shards, -0.22, 0.18)
    return jnp.clip(values, -bound, bound).astype(dtype)


def setup_inputs(seed: int = 0) -> dict:
    keys = jax.random.split(jax.random.key(seed), 7)
    slopes = bell_draw(keys[0], (TOTAL_FRAMES, SENSOR_SLOPES), 1.0, 6.0, ((0, 512),))
    reconstructor = bell_draw(keys[1], (SENSOR_SLOPES, STATE_MODES), SENSOR_SLOPES ** -0.5, 0.1875, ((0, 8),))
    interaction = bell_draw(keys[2], (STATE_MODES, SENSOR_SLOPES), STATE_MODES ** -0.5, 0.25, ((1, 8),))
    frame_valid = with_ends((jax.random.randint(keys[3], (NBLK,), 0, 4) < 3).astype(jnp.int32), jax.random.fold_in(keys[3], 1), 0, 1)
    open_rate = draw_open_rate(jax.random.fold_in(keys[6], 71), 0)
    closed_rate = draw_closed_rate(jax.random.fold_in(keys[6], 71), 0)
    return dict(slopes=slopes, reconstructor=reconstructor, interaction=interaction, frame_valid=frame_valid, open_rate=open_rate, closed_rate=closed_rate)


def reference(slopes, reconstructor, interaction, frame_valid, open_rate, closed_rate):
    frame_blocks = TOTAL_FRAMES // BLOCK_FRAMES
    blocked_slopes = slopes.reshape(frame_blocks, BLOCK_FRAMES, SENSOR_SLOPES)
    gain = 1.0 - jnp.exp(open_rate - closed_rate)
    inject = gain / jnp.sqrt(2.0 * closed_rate)

    def forward(state, inputs):
        block_slopes, flag = inputs
        modal = jnp.dot(block_slopes, reconstructor, preferred_element_type=jnp.float32)
        validf = flag.astype(jnp.float32)
        factor = jnp.exp(-jnp.where(validf > 0.5, closed_rate, open_rate))
        offsets = validf * inject * modal

        def frame(inner, offset):
            following = factor * inner + offset
            return (following, following)
        state, states = lax.scan(frame, state, offsets)
        return (state, states)
    _, filtered = lax.scan(forward, jnp.zeros((STATE_MODES,), jnp.float32), (blocked_slopes, frame_valid))
    filtered = filtered.reshape(TOTAL_FRAMES, STATE_MODES)
    keep = jnp.exp(-closed_rate)
    blend = 1.0 - keep * jnp.exp(-open_rate)

    def backward(following, current):
        value = keep * following + blend * current
        return (value, value)
    _, earlier = lax.scan(backward, filtered[-1], filtered[:-1], reverse=True)
    smoothed = jnp.concatenate([earlier, filtered[-1:]], axis=0).astype(jnp.bfloat16)
    smoothed_blocks = smoothed.reshape(frame_blocks, BLOCK_FRAMES, STATE_MODES)

    def project_modes(inputs):
        block_slopes, block_state = inputs
        fitted = jnp.dot(block_state, interaction, preferred_element_type=jnp.float32)
        return (block_slopes.astype(jnp.float32) - fitted).astype(jnp.bfloat16)
    residual = lax.map(project_modes, (blocked_slopes, smoothed_blocks)).reshape(TOTAL_FRAMES, SENSOR_SLOPES)
    return (smoothed, residual)
```

```python
import functools

import jax
import jax.numpy as jnp
from jax import lax
from jax.experimental import pallas as pl
from jax.experimental.pallas import tpu as pltpu
from jax.sharding import PartitionSpec as P

MESH = pl.DeviceIdType.MESH
F32 = jnp.float32
LANES = 128
ROWS = 8


def one_minus_exp(x):
    series = x * (1 - x / 2 * (1 - x / 3 * (1 - x / 4 * (1 - x / 5 * (1 - x / 6)))))
    return jnp.where(x < 0.1, series, 1.0 - jnp.exp(-x))


def kernel(
    n_y, n_z, n_x,
    slopes_ref, recon_ref, inter_ref, valid_ref, open_ref, closed_ref,
    smooth_ref, resid_ref,
    rbuf, ibuf, modal, state0, back_in, fwd_in, cst, rates, carry, st1, st2, st3,
    own_sem, r_send, r_recv, i_send, i_recv, e_send, e_recv,
):
    frames = slopes_ref.shape[0]
    modes = recon_ref.shape[1]
    tiles = modes // LANES
    blocks = frames // ROWS
    grp = lax.axis_index("grp")
    span = lax.axis_index("span")
    y, z = grp // n_z, grp % n_z
    x, core = span // 2, span % 2
    n_span = 2 * n_x
    other = x * 2 + (1 - core)
    right = ((x + 1) % n_x) * 2 + core
    left = ((x + n_x - 1) % n_x) * 2 + core

    span_peers = [{"span": (span + k) % n_span} for k in range(1, n_span)]
    z_peers = [{"grp": y * n_z + (z + k) % n_z} for k in range(1, n_z)]
    y_peers = [{"grp": ((y + k) % n_y) * n_z + z} for k in range(1, n_y)]

    barrier = pltpu.get_barrier_semaphore()
    everyone = span_peers + z_peers + y_peers
    for peer in everyone:
        pl.semaphore_signal(barrier, inc=1, device_id=peer, device_id_type=MESH)

    half_r, half_i = recon_ref.shape[0] // 2, inter_ref.shape[0] // 2

    def r_slot(j, c, h):
        if h is None:
            return rbuf.at[j, c]
        return rbuf.at[j, c, pl.ds(h * half_r, half_r), :]

    def r_own(h):
        return recon_ref if h is None else recon_ref.at[pl.ds(h * half_r, half_r), :]

    def i_slot(j, c, h):
        cols = pl.ds(pl.multiple_of(c * LANES, LANES), LANES)
        if h is None:
            return ibuf.at[j, :, cols]
        return ibuf.at[j, pl.ds(h * half_i, half_i), cols]

    def i_own(h):
        return inter_ref if h is None else inter_ref.at[pl.ds(h * half_i, half_i), :]

    class Gather:
        def __init__(self, slot, own, send, recv):
            self.slot, self.own, self.send, self.recv = slot, own, send, recv
            self.started = []

        def push(self, n, src, dst, to):
            copy = pltpu.make_async_remote_copy(
                src_ref=src, dst_ref=dst, send_sem=self.send.at[n], recv_sem=self.recv.at[n],
                device_id={"span": to}, device_id_type=MESH,
            )
            copy.start()
            self.started.append(copy)

        def arrived(self, n, where):
            pltpu.make_async_remote_copy(
                src_ref=where, dst_ref=where, send_sem=self.send.at[n], recv_sem=self.recv.at[n],
                device_id={"span": other}, device_id_type=MESH,
            ).wait_recv()

        def begin(self):
            slot, own = self.slot, self.own
            self.push(0, own(0), slot(3, core, 0), right)
            self.push(2, own(1), slot(1, core, 1), left)
            self.push(1, own(1), slot(3, core, 1), right)
            self.push(3, own(0), slot(1, core, 0), left)
            self.push(6, own(None), slot(0, core, None), other)

        def relay_first(self):
            slot = self.slot
            self.arrived(0, slot(3, core, 0))
            self.push(4, slot(3, core, 0), slot(2, core, 0), right)
            self.push(7, slot(3, core, 0), slot(3, core, 0), other)
            self.arrived(2, slot(1, core, 1))
            self.push(5, slot(1, core, 1), slot(2, core, 1), left)
            self.push(9, slot(1, core, 1), slot(1, core, 1), other)

        def relay_second(self):
            slot = self.slot
            self.arrived(1, slot(3, core, 1))
            self.push(8, slot(3, core, 1), slot(3, core, 1), other)
            self.arrived(3, slot(1, core, 0))
            self.push(10, slot(1, core, 0), slot(1, core, 0), other)

        def relay_third(self):
            slot = self.slot
            self.arrived(4, slot(2, core, 0))
            self.push(11, slot(2, core, 0), slot(2, core, 0), other)
            self.arrived(5, slot(2, core, 1))
            self.push(12, slot(2, core, 1), slot(2, core, 1), other)

        def wait_chip(self, j):
            there, slot = 1 - core, self.slot
            for n, h in {0: [(6, None)], 3: [(7, 0), (8, 1)], 1: [(9, 1), (10, 0)],
                         2: [(11, 0), (12, 1)]}[j]:
                self.arrived(n, slot(j, there, h))

        def drain(self):
            for copy in self.started:
                copy.wait_send()

    recon = Gather(r_slot, r_own, r_send, r_recv)
    inter = Gather(i_slot, i_own, i_send, i_recv)
    keep_r = pltpu.make_async_copy(recon_ref, r_slot(0, core, None), own_sem.at[0])
    keep_i = pltpu.make_async_copy(inter_ref, i_slot(0, core, None), own_sem.at[1])
    keep_r.start()
    keep_i.start()

    pl.semaphore_wait(barrier, len(everyone))
    recon.begin()

    row = lax.broadcasted_iota(jnp.int32, (ROWS, LANES), 0)
    rowf = row.astype(F32)
    flag = valid_ref[0].astype(F32)

    def lane(l):
        return pl.ds(l * LANES, LANES)

    def back_scan(source, target, l):
        q1, q2, q4, qw, k8 = (cst[l, n] for n in range(5, 10))
        blend = cst[l, 11]
        parts = []
        for k in range(blocks):
            v = blend * source(k)
            v = v + q1 * pltpu.roll(v, ROWS - 1, 0)
            v = v + q2 * pltpu.roll(v, ROWS - 2, 0)
            v = v + q4 * pltpu.roll(v, ROWS - 4, 0)
            parts.append(v)
        after = jnp.zeros((ROWS, LANES), F32)
        for k in reversed(range(blocks)):
            target[pl.ds(k * ROWS, ROWS), lane(l)] = parts[k] + qw * after
            after = k8 * after + jnp.broadcast_to(parts[k][0:1], (ROWS, LANES))
        return after[0:1]

    for l in range(tiles):
        a_rate = jnp.broadcast_to(open_ref[:, lane(l)], (ROWS, LANES))
        c_rate = jnp.broadcast_to(closed_ref[:, lane(l)], (ROWS, LANES))
        rates[pl.ds(l, 1), :] = open_ref[:, lane(l)]
        rates[pl.ds(tiles + l, 1), :] = closed_ref[:, lane(l)]
        rate = jnp.where(jnp.full((ROWS, LANES), flag) > 0.5, c_rate, a_rate)
        for n, d in enumerate((1, 2, 4)):
            cst[l, n] = jnp.where(row >= d, jnp.exp(-d * rate), 0.0)
            cst[l, 5 + n] = jnp.where(row < ROWS - d, jnp.exp(-d * c_rate), 0.0)
        pw = jnp.exp(-(rowf + 1.0) * rate)
        cst[l, 3] = pw
        cst[l, 4] = jnp.exp(-float(ROWS) * rate)
        cst[l, 8] = jnp.exp(-(float(ROWS) - rowf) * c_rate)
        cst[l, 9] = jnp.exp(-float(ROWS) * c_rate)
        gain = one_minus_exp(c_rate - a_rate)
        cst[l, 10] = flag * (gain / jnp.sqrt(2.0 * c_rate))
        cst[l, 11] = one_minus_exp(a_rate + c_rate)
        for k in range(blocks):
            back_in[pl.ds(k * ROWS, ROWS), lane(l)] = jnp.exp(
                -(float(frames - k * ROWS) - rowf) * c_rate
            )
        first = back_scan(lambda k: jnp.exp(-(rowf + float(k * ROWS + 1)) * rate), fwd_in, l)
        st1[span, pl.ds(2 * tiles + l, 1), :] = first
        st1[span, pl.ds(l, 1), :] = jnp.exp(-float(frames) * rate[0:1])

    closed4 = rates[pl.ds(tiles, tiles), :]
    decay4 = jnp.exp(-rates[pl.ds(0, tiles), :])

    def modal_part(j):
        cols = pl.ds(pl.multiple_of(((x + j) % n_x) * 2 * LANES, 2 * LANES), 2 * LANES)
        return jnp.dot(
            slopes_ref[:, cols], rbuf[j].reshape(2 * LANES, modes), preferred_element_type=F32
        )

    keep_r.wait()
    recon.wait_chip(0)
    modal[...] = modal_part(0)
    recon.relay_first()
    recon.relay_second()
    recon.wait_chip(3)
    modal[...] += modal_part(3)
    recon.wait_chip(1)
    modal[...] += modal_part(1)
    recon.relay_third()
    recon.wait_chip(2)
    modal[...] += modal_part(2)

    for l in range(tiles):
        p1, p2, p4, pw, f8 = (cst[l, n] for n in range(5))
        inject = cst[l, 10]
        parts = []
        for k in range(blocks):
            v = inject * modal[pl.ds(k * ROWS, ROWS), lane(l)]
            v = v + p1 * pltpu.roll(v, 1, 0)
            v = v + p2 * pltpu.roll(v, 2, 0)
            v = v + p4 * pltpu.roll(v, 4, 0)
            parts.append(v)
        before = jnp.zeros((ROWS, LANES), F32)
        filtered = []
        for k in range(blocks):
            filtered.append(parts[k] + pw * before)
            before = f8 * before + jnp.broadcast_to(parts[k][ROWS - 1:], (ROWS, LANES))
        first = back_scan(lambda k: filtered[k], state0, l)
        st1[span, pl.ds(tiles + l, 1), :] = before[0:1]
        st1[span, pl.ds(3 * tiles + l, 1), :] = first

    def spread(stage, buf, me, peers, base):
        copies = []
        for n, peer in enumerate(peers):
            copy = pltpu.make_async_remote_copy(
                src_ref=buf.at[me], dst_ref=buf.at[me],
                send_sem=e_send.at[base + n], recv_sem=e_recv.at[base + n],
                device_id=peer, device_id_type=MESH,
            )
            copy.start()
            copies.append(copy)
        return copies

    def collect(buf, me, count, peers, base):
        for n, peer in enumerate(peers):
            slot = buf.at[(me + count - 1 - n) % count]
            pltpu.make_async_remote_copy(
                src_ref=slot, dst_ref=slot,
                send_sem=e_send.at[base + n], recv_sem=e_recv.at[base + n],
                device_id=peer, device_id_type=MESH,
            ).wait_recv()

    def element(buf, k):
        return tuple(buf[k, pl.ds(q * tiles, tiles), :] for q in range(4))

    def total(buf, count, length):
        thr, end, resp, start = element(buf, 0)
        for k in range(1, count):
            thr_k, end_k, resp_k, start_k = element(buf, k)
            psi = jnp.exp(-float(k * length) * closed4)
            start = start + psi * (start_k + resp_k * end)
            resp = resp + psi * resp_k * thr
            end = thr_k * end + end_k
            thr = thr * thr_k
        return thr, end, resp, start

    def put(buf, me, parts):
        for q in range(4):
            buf[me, pl.ds(q * tiles, tiles), :] = parts[q]

    def solve(buf, me, count, length, before, after):
        psi = jnp.exp(-float(length) * closed4)
        entering = [before]
        for k in range(count):
            thr, end, _, _ = element(buf, k)
            entering.append(thr * entering[k] + end)
        state = decay4 * entering[count] if after is None else after
        mine_in, mine_after = entering[0], state
        for k in range(1, count):
            mine_in = jnp.where(me == k, entering[k], mine_in)
        for k in range(count - 1, 0, -1):
            _, _, resp, start = element(buf, k)
            state = psi * state + resp * entering[k] + start
            mine_after = jnp.where(me == k - 1, state, mine_after)
        return mine_in, mine_after

    sent = spread(0, st1, span, span_peers, 0)
    inter.begin()
    collect(st1, span, n_span, span_peers, 0)
    put(st2, z, total(st1, n_span, frames))
    base_z = n_span - 1
    sent += spread(1, st2, z, z_peers, base_z)
    inter.relay_first()
    inter.relay_second()
    collect(st2, z, n_z, z_peers, base_z)
    put(st3, y, total(st2, n_z, n_span * frames))
    base_y = base_z + n_z - 1
    sent += spread(2, st3, y, y_peers, base_y)
    inter.relay_third()
    collect(st3, y, n_y, y_peers, base_y)

    before = jnp.zeros((tiles, LANES), F32)
    before, after = solve(st3, y, n_y, n_z * n_span * frames, before, None)
    before, after = solve(st2, z, n_z, n_span * frames, before, after)
    before, after = solve(st1, span, n_span, frames, before, after)
    carry[pl.ds(0, tiles), :] = before
    carry[pl.ds(tiles, tiles), :] = after
    for l in range(tiles):
        state = (
            state0[:, lane(l)]
            + back_in[:, lane(l)] * carry[pl.ds(tiles + l, 1), :]
            + fwd_in[:, lane(l)] * carry[pl.ds(l, 1), :]
        )
        smooth_ref[:, lane(l)] = state.astype(jnp.bfloat16)

    keep_i.wait()
    for j in (0, 3, 1, 2):
        inter.wait_chip(j)
        cols = pl.ds(pl.multiple_of(((x + j) % n_x) * 2 * LANES, 2 * LANES), 2 * LANES)
        fitted = jnp.dot(smooth_ref[...], ibuf[j], preferred_element_type=F32)
        resid_ref[:, cols] = (slopes_ref[:, cols].astype(F32) - fitted).astype(jnp.bfloat16)

    recon.drain()
    inter.drain()
    for copy in sent:
        copy.wait_send()


def body(n_y, n_z, n_x, slopes, reconstructor, interaction, frame_valid, open_rate, closed_rate):
    frames, n_slopes = slopes.shape
    modes = reconstructor.shape[1]
    tiles = modes // LANES
    n_span = 2 * n_x
    messages = n_span - 1 + n_z - 1 + n_y - 1
    vmem = pl.BlockSpec(memory_space=pltpu.VMEM)
    whole = (frames, modes)
    return pl.pallas_call(
        functools.partial(kernel, n_y, n_z, n_x),
        out_shape=(
            jax.ShapeDtypeStruct((frames, modes), jnp.bfloat16),
            jax.ShapeDtypeStruct((frames, n_slopes), jnp.bfloat16),
        ),
        in_specs=[vmem, vmem, vmem, pl.BlockSpec(memory_space=pltpu.SMEM), vmem, vmem],
        out_specs=(vmem, vmem),
        scratch_shapes=[
            pltpu.VMEM((n_x, 2, LANES, modes), jnp.bfloat16),
            pltpu.VMEM((n_x, modes, 2 * LANES), jnp.bfloat16),
            pltpu.VMEM(whole, F32),
            pltpu.VMEM(whole, F32),
            pltpu.VMEM(whole, F32),
            pltpu.VMEM(whole, F32),
            pltpu.VMEM((tiles, 12, ROWS, LANES), F32),
            pltpu.VMEM((2 * tiles, LANES), F32),
            pltpu.VMEM((2 * tiles, LANES), F32),
            pltpu.VMEM((n_span, 4 * tiles, LANES), F32),
            pltpu.VMEM((n_z, 4 * tiles, LANES), F32),
            pltpu.VMEM((n_y, 4 * tiles, LANES), F32),
            pltpu.SemaphoreType.DMA((2,)),
            pltpu.SemaphoreType.DMA((13,)),
            pltpu.SemaphoreType.DMA((13,)),
            pltpu.SemaphoreType.DMA((13,)),
            pltpu.SemaphoreType.DMA((13,)),
            pltpu.SemaphoreType.DMA((messages,)),
            pltpu.SemaphoreType.DMA((messages,)),
        ],
        compiler_params=pltpu.CompilerParams(collective_id=0, has_side_effects=True),
    )(
        slopes, reconstructor, interaction, frame_valid,
        open_rate.reshape(1, modes), closed_rate.reshape(1, modes),
    )


def solution(mesh):
    grp, span = mesh.shape["grp"], mesh.shape["span"]
    n_z = 8 if grp % 8 == 0 else 1
    in_specs = (
        P(("grp", "span"), None),
        P("span", None),
        P(None, "span"),
        P(("grp", "span")),
        P(),
        P(),
    )
    out_specs = (P(("grp", "span"), None), P(("grp", "span"), None))
    return jax.shard_map(
        functools.partial(body, grp // n_z, n_z, span // 2),
        mesh=mesh, in_specs=in_specs, out_specs=out_specs, check_vma=False,
    )
```

```python
import functools

import jax
import jax.numpy as jnp
from jax import lax
from jax.experimental import pallas as pl
from jax.experimental.pallas import tpu as pltpu
from jax.sharding import PartitionSpec as P

MESH = pl.DeviceIdType.MESH
F32 = jnp.float32
LANES = 128
ROWS = 8


def one_minus_exp(x):
    series = x * (1 - x / 2 * (1 - x / 3 * (1 - x / 4 * (1 - x / 5 * (1 - x / 6)))))
    return jnp.where(x < 0.1, series, 1.0 - jnp.exp(-x))


def kernel(
    n_y, n_z, n_x,
    slopes_hbm, recon_ref, inter_ref, valid_ref, open_ref, closed_ref,
    smooth_hbm, resid_hbm,
    slopes_ref, smooth_ref, resid_ref,
    rbuf, ibuf, modal, state0, back_in, fwd_in, cst, rates, carry,
    a1, a2, a3, b1, b2, b3,
    own_sem, out_sem, r_send, r_recv, i_send, i_recv, e_send, e_recv,
):
    frames = slopes_ref.shape[0]
    modes = recon_ref.shape[1]
    tiles = modes // LANES
    blocks = frames // ROWS
    grp = lax.axis_index("grp")
    span = lax.axis_index("span")
    y, z = grp // n_z, grp % n_z
    x, core = span // 2, span % 2
    n_span = 2 * n_x
    other = x * 2 + (1 - core)
    right = ((x + 1) % n_x) * 2 + core
    left = ((x + n_x - 1) % n_x) * 2 + core

    span_peers = [{"span": (span + k) % n_span} for k in range(1, n_span)]
    z_peers = [{"grp": y * n_z + (z + k) % n_z} for k in range(1, n_z)]
    y_peers = [{"grp": ((y + k) % n_y) * n_z + z} for k in range(1, n_y)]

    barrier = pltpu.get_barrier_semaphore()
    everyone = span_peers + z_peers + y_peers
    for peer in everyone:
        pl.semaphore_signal(barrier, inc=1, device_id=peer, device_id_type=MESH)

    half_r, half_i = recon_ref.shape[0] // 2, inter_ref.shape[0] // 2

    def r_slot(j, c, h):
        if h is None:
            return rbuf.at[j, c]
        return rbuf.at[j, c, pl.ds(h * half_r, half_r), :]

    def r_own(h):
        return recon_ref if h is None else recon_ref.at[pl.ds(h * half_r, half_r), :]

    def i_slot(j, c, h):
        cols = pl.ds(pl.multiple_of(c * LANES, LANES), LANES)
        if h is None:
            return ibuf.at[j, :, cols]
        return ibuf.at[j, pl.ds(h * half_i, half_i), cols]

    def i_own(h):
        return inter_ref if h is None else inter_ref.at[pl.ds(h * half_i, half_i), :]

    class Gather:
        def __init__(self, slot, own, send, recv):
            self.slot, self.own, self.send, self.recv = slot, own, send, recv
            self.started = []

        def push(self, n, src, dst, to):
            copy = pltpu.make_async_remote_copy(
                src_ref=src, dst_ref=dst, send_sem=self.send.at[n], recv_sem=self.recv.at[n],
                device_id={"span": to}, device_id_type=MESH,
            )
            copy.start()
            self.started.append(copy)

        def arrived(self, n, where):
            pltpu.make_async_remote_copy(
                src_ref=where, dst_ref=where, send_sem=self.send.at[n], recv_sem=self.recv.at[n],
                device_id={"span": other}, device_id_type=MESH,
            ).wait_recv()

        def begin(self):
            slot, own = self.slot, self.own
            self.push(0, own(0), slot(3, core, 0), right)
            self.push(2, own(1), slot(1, core, 1), left)
            self.push(1, own(1), slot(3, core, 1), right)
            self.push(3, own(0), slot(1, core, 0), left)
            self.push(6, own(None), slot(0, core, None), other)

        def relay_first(self):
            slot = self.slot
            self.arrived(0, slot(3, core, 0))
            self.push(4, slot(3, core, 0), slot(2, core, 0), right)
            self.push(7, slot(3, core, 0), slot(3, core, 0), other)
            self.arrived(2, slot(1, core, 1))
            self.push(5, slot(1, core, 1), slot(2, core, 1), left)
            self.push(9, slot(1, core, 1), slot(1, core, 1), other)

        def relay_second(self):
            slot = self.slot
            self.arrived(1, slot(3, core, 1))
            self.push(8, slot(3, core, 1), slot(3, core, 1), other)
            self.arrived(3, slot(1, core, 0))
            self.push(10, slot(1, core, 0), slot(1, core, 0), other)

        def relay_third(self):
            slot = self.slot
            self.arrived(4, slot(2, core, 0))
            self.push(11, slot(2, core, 0), slot(2, core, 0), other)
            self.arrived(5, slot(2, core, 1))
            self.push(12, slot(2, core, 1), slot(2, core, 1), other)

        def wait_chip(self, j):
            there, slot = 1 - core, self.slot
            for n, h in {0: [(6, None)], 3: [(7, 0), (8, 1)], 1: [(9, 1), (10, 0)],
                         2: [(11, 0), (12, 1)]}[j]:
                self.arrived(n, slot(j, there, h))

        def drain(self):
            for copy in self.started:
                copy.wait_send()

    recon = Gather(r_slot, r_own, r_send, r_recv)
    inter = Gather(i_slot, i_own, i_send, i_recv)
    keep_r = pltpu.make_async_copy(recon_ref, r_slot(0, core, None), own_sem.at[0])
    keep_i = pltpu.make_async_copy(inter_ref, i_slot(0, core, None), own_sem.at[1])
    keep_s = pltpu.make_async_copy(slopes_hbm, slopes_ref, own_sem.at[2])

    pl.semaphore_wait(barrier, len(everyone))
    recon.begin()
    keep_r.start()
    keep_s.start()
    keep_i.start()

    row = lax.broadcasted_iota(jnp.int32, (ROWS, LANES), 0)
    rowf = row.astype(F32)
    flag = jnp.broadcast_to(valid_ref[...].astype(F32), (ROWS, LANES))

    def lane(l):
        return pl.ds(l * LANES, LANES)

    def back_scan(source, target, l):
        q1, q2, q4, qw, k8 = (cst[l, n] for n in range(5, 10))
        blend = cst[l, 11]
        parts = []
        for k in range(blocks):
            v = blend * source(k)
            v = v + q1 * pltpu.roll(v, ROWS - 1, 0)
            v = v + q2 * pltpu.roll(v, ROWS - 2, 0)
            v = v + q4 * pltpu.roll(v, ROWS - 4, 0)
            parts.append(v)
        after = jnp.zeros((ROWS, LANES), F32)
        for k in reversed(range(blocks)):
            target[pl.ds(k * ROWS, ROWS), lane(l)] = parts[k] + qw * after
            after = k8 * after + jnp.broadcast_to(parts[k][0:1], (ROWS, LANES))
        return after[0:1]

    for l in range(tiles):
        a_rate = jnp.broadcast_to(open_ref[:, lane(l)], (ROWS, LANES))
        c_rate = jnp.broadcast_to(closed_ref[:, lane(l)], (ROWS, LANES))
        rates[pl.ds(l, 1), :] = open_ref[:, lane(l)]
        rates[pl.ds(tiles + l, 1), :] = closed_ref[:, lane(l)]
        rate = jnp.where(flag > 0.5, c_rate, a_rate)
        for n, d in enumerate((1, 2, 4)):
            cst[l, n] = jnp.where(row >= d, jnp.exp(-d * rate), 0.0)
            cst[l, 5 + n] = jnp.where(row < ROWS - d, jnp.exp(-d * c_rate), 0.0)
        pw = jnp.exp(-(rowf + 1.0) * rate)
        cst[l, 3] = pw
        cst[l, 4] = jnp.exp(-float(ROWS) * rate)
        cst[l, 8] = jnp.exp(-(float(ROWS) - rowf) * c_rate)
        cst[l, 9] = jnp.exp(-float(ROWS) * c_rate)
        gain = one_minus_exp(c_rate - a_rate)
        cst[l, 10] = flag * (gain / jnp.sqrt(2.0 * c_rate))
        cst[l, 11] = one_minus_exp(a_rate + c_rate)
        for k in range(blocks):
            back_in[pl.ds(k * ROWS, ROWS), lane(l)] = jnp.exp(
                -(float(frames - k * ROWS) - rowf) * c_rate
            )
        first = back_scan(lambda k: jnp.exp(-(rowf + float(k * ROWS + 1)) * rate), fwd_in, l)
        a1[span, pl.ds(tiles + l, 1), :] = first
        a1[span, pl.ds(l, 1), :] = jnp.exp(-float(frames) * rate[0:1])

    closed4 = rates[pl.ds(tiles, tiles), :]
    decay4 = jnp.exp(-rates[pl.ds(0, tiles), :])

    def exchange(buf, me, peers, base):
        for n, peer in enumerate(peers):
            copy = pltpu.make_async_remote_copy(
                src_ref=buf.at[me], dst_ref=buf.at[me],
                send_sem=e_send.at[base + n], recv_sem=e_recv.at[base + n],
                device_id=peer, device_id_type=MESH,
            )
            copy.start()
            sent.append(copy)

    def collect(buf, me, peers, base):
        count = len(peers) + 1
        for n, peer in enumerate(peers):
            slot = buf.at[(me + count - 1 - n) % count]
            pltpu.make_async_remote_copy(
                src_ref=slot, dst_ref=slot,
                send_sem=e_send.at[base + n], recv_sem=e_recv.at[base + n],
                device_id=peer, device_id_type=MESH,
            ).wait_recv()

    def pair(buf, k):
        return buf[k, pl.ds(0, tiles), :], buf[k, pl.ds(tiles, tiles), :]

    def put(buf, me, parts):
        for q in range(2):
            buf[me, pl.ds(q * tiles, tiles), :] = parts[q]

    def psi(n):
        return jnp.exp(-float(n) * closed4)

    def total_a(a, count, length):
        thr, resp = pair(a, 0)
        for k in range(1, count):
            thr_k, resp_k = pair(a, k)
            resp = resp + psi(k * length) * resp_k * thr
            thr = thr * thr_k
        return thr, resp

    def total_b(a, b, count, length):
        end, start = pair(b, 0)
        for k in range(1, count):
            (thr_k, resp_k), (end_k, start_k) = pair(a, k), pair(b, k)
            start = start + psi(k * length) * (start_k + resp_k * end)
            end = thr_k * end + end_k
        return end, start

    def affine(a, b, me, count, length):
        thr, end = jnp.ones((tiles, LANES), F32), jnp.zeros((tiles, LANES), F32)
        thr_in, end_in = thr, end
        for k in range(count):
            (thr_k, _), (end_k, _) = pair(a, k), pair(b, k)
            thr_in, end_in = jnp.where(me == k, thr, thr_in), jnp.where(me == k, end, end_in)
            thr, end = jnp.where(k <= me, thr * thr_k, thr), jnp.where(k <= me, thr_k * end + end_k, end)
        step = psi(length)
        resp, start = jnp.zeros((tiles, LANES), F32), jnp.zeros((tiles, LANES), F32)
        far = jnp.ones((tiles, LANES), F32)
        for k in range(count - 1, 0, -1):
            (thr_k, resp_k), (end_k, start_k) = pair(a, k), pair(b, k)
            start = jnp.where(k > me, start_k + step * (start + resp * end_k), start)
            resp = jnp.where(k > me, resp_k + step * resp * thr_k, resp)
            far = jnp.where(k > me, far * step, far)
        return thr_in, end_in, far, resp * thr, resp * end + start

    def apply(form, before, after):
        thr_in, end_in, far, resp, start = form
        return thr_in * before + end_in, far * after + resp * before + start

    def solve_top(a, b, me, count, length):
        step = psi(length)
        entering = [jnp.zeros((tiles, LANES), F32)]
        for k in range(count):
            (thr_k, _), (end_k, _) = pair(a, k), pair(b, k)
            entering.append(thr_k * entering[k] + end_k)
        state = decay4 * entering[count]
        mine_in, mine_after = entering[0], state
        for k in range(1, count):
            mine_in = jnp.where(me == k, entering[k], mine_in)
        for k in range(count - 1, 0, -1):
            (_, resp_k), (_, start_k) = pair(a, k), pair(b, k)
            state = step * state + resp_k * entering[k] + start_k
            mine_after = jnp.where(me == k - 1, state, mine_after)
        return mine_in, mine_after

    sent = []
    base_z = n_span - 1
    base_y = base_z + n_z - 1
    late = base_y + n_y - 1
    len_z, len_y = n_span * frames, n_z * n_span * frames
    exchange(a1, span, span_peers, 0)

    def modal_part(j):
        cols = pl.ds(pl.multiple_of(((x + j) % n_x) * 2 * LANES, 2 * LANES), 2 * LANES)
        return jnp.dot(
            slopes_ref[:, cols], rbuf[j].reshape(2 * LANES, modes), preferred_element_type=F32
        )

    keep_r.wait()
    keep_s.wait()
    recon.wait_chip(0)
    modal[...] = modal_part(0)
    recon.relay_first()
    recon.relay_second()
    recon.wait_chip(3)
    modal[...] += modal_part(3)
    collect(a1, span, span_peers, 0)
    put(a2, z, total_a(a1, n_span, frames))
    exchange(a2, z, z_peers, base_z)
    recon.wait_chip(1)
    modal[...] += modal_part(1)
    recon.relay_third()
    recon.wait_chip(2)
    modal[...] += modal_part(2)

    for l in range(tiles):
        p1, p2, p4, pw, f8 = (cst[l, n] for n in range(5))
        inject = cst[l, 10]
        parts = []
        for k in range(blocks):
            v = inject * modal[pl.ds(k * ROWS, ROWS), lane(l)]
            v = v + p1 * pltpu.roll(v, 1, 0)
            v = v + p2 * pltpu.roll(v, 2, 0)
            v = v + p4 * pltpu.roll(v, 4, 0)
            parts.append(v)
        before = jnp.zeros((ROWS, LANES), F32)
        filtered = []
        for k in range(blocks):
            filtered.append(parts[k] + pw * before)
            before = f8 * before + jnp.broadcast_to(parts[k][ROWS - 1:], (ROWS, LANES))
        first = back_scan(lambda k: filtered[k], state0, l)
        b1[span, pl.ds(l, 1), :] = before[0:1]
        b1[span, pl.ds(tiles + l, 1), :] = first

    exchange(b1, span, span_peers, late)
    inter.begin()
    collect(b1, span, span_peers, late)
    put(b2, z, total_b(a1, b1, n_span, frames))
    exchange(b2, z, z_peers, late + base_z)
    collect(a2, z, z_peers, base_z)
    put(a3, y, total_a(a2, n_z, len_z))
    exchange(a3, y, y_peers, base_y)
    inter.relay_first()
    inter.relay_second()
    form_x = affine(a1, b1, span, n_span, frames)
    collect(b2, z, z_peers, late + base_z)
    put(b3, y, total_b(a2, b2, n_z, len_z))
    exchange(b3, y, y_peers, late + base_y)
    inter.relay_third()
    form_z = affine(a2, b2, z, n_z, len_z)
    collect(a3, y, y_peers, base_y)
    collect(b3, y, y_peers, late + base_y)

    before, after = solve_top(a3, b3, y, n_y, len_y)
    before, after = apply(form_z, before, after)
    before, after = apply(form_x, before, after)
    carry[pl.ds(0, tiles), :] = before
    carry[pl.ds(tiles, tiles), :] = after
    for l in range(tiles):
        state = (
            state0[:, lane(l)]
            + back_in[:, lane(l)] * carry[pl.ds(tiles + l, 1), :]
            + fwd_in[:, lane(l)] * carry[pl.ds(l, 1), :]
        )
        smooth_ref[:, lane(l)] = state.astype(jnp.bfloat16)
    outs = [pltpu.make_async_copy(smooth_ref, smooth_hbm, out_sem.at[0])]
    outs[0].start()

    keep_i.wait()
    for j in (0, 3, 1, 2):
        inter.wait_chip(j)
        cols = pl.ds(pl.multiple_of(((x + j) % n_x) * 2 * LANES, 2 * LANES), 2 * LANES)
        fitted = jnp.dot(smooth_ref[...], ibuf[j], preferred_element_type=F32)
        resid_ref[:, cols] = (slopes_ref[:, cols].astype(F32) - fitted).astype(jnp.bfloat16)
        outs.append(
            pltpu.make_async_copy(resid_ref.at[:, cols], resid_hbm.at[:, cols], out_sem.at[1 + j])
        )
        outs[-1].start()

    recon.drain()
    inter.drain()
    for copy in sent:
        copy.wait_send()
    for copy in outs:
        copy.wait()


def body(n_y, n_z, n_x, slopes, reconstructor, interaction, frame_valid, open_rate, closed_rate):
    frames, n_slopes = slopes.shape
    modes = reconstructor.shape[1]
    tiles = modes // LANES
    n_span = 2 * n_x
    messages = 2 * (n_span - 1 + n_z - 1 + n_y - 1)
    hbm = pl.BlockSpec(memory_space=pl.ANY)
    vmem = pl.BlockSpec(memory_space=pltpu.VMEM)
    whole = (frames, modes)
    return pl.pallas_call(
        functools.partial(kernel, n_y, n_z, n_x),
        out_shape=(
            jax.ShapeDtypeStruct((frames, modes), jnp.bfloat16),
            jax.ShapeDtypeStruct((frames, n_slopes), jnp.bfloat16),
        ),
        in_specs=[hbm, hbm, hbm, vmem, vmem, vmem],
        out_specs=(hbm, hbm),
        scratch_shapes=[
            pltpu.VMEM((frames, n_slopes), jnp.bfloat16),
            pltpu.VMEM(whole, jnp.bfloat16),
            pltpu.VMEM((frames, n_slopes), jnp.bfloat16),
            pltpu.VMEM((n_x, 2, LANES, modes), jnp.bfloat16),
            pltpu.VMEM((n_x, modes, 2 * LANES), jnp.bfloat16),
            pltpu.VMEM(whole, F32),
            pltpu.VMEM(whole, F32),
            pltpu.VMEM(whole, F32),
            pltpu.VMEM(whole, F32),
            pltpu.VMEM((tiles, 12, ROWS, LANES), F32),
            pltpu.VMEM((2 * tiles, LANES), F32),
            pltpu.VMEM((2 * tiles, LANES), F32),
            *[pltpu.VMEM((n, 2 * tiles, LANES), F32) for n in (n_span, n_z, n_y) * 2],
            pltpu.SemaphoreType.DMA((3,)),
            pltpu.SemaphoreType.DMA((1 + n_x,)),
            pltpu.SemaphoreType.DMA((13,)),
            pltpu.SemaphoreType.DMA((13,)),
            pltpu.SemaphoreType.DMA((13,)),
            pltpu.SemaphoreType.DMA((13,)),
            pltpu.SemaphoreType.DMA((messages,)),
            pltpu.SemaphoreType.DMA((messages,)),
        ],
        compiler_params=pltpu.CompilerParams(collective_id=0, has_side_effects=True),
    )(
        slopes, reconstructor, interaction, frame_valid.reshape(1, 1),
        open_rate.reshape(1, modes), closed_rate.reshape(1, modes),
    )


def solution(mesh):
    grp, span = mesh.shape["grp"], mesh.shape["span"]
    n_z = 8 if grp % 8 == 0 else 1
    in_specs = (
        P(("grp", "span"), None),
        P("span", None),
        P(None, "span"),
        P(("grp", "span")),
        P(),
        P(),
    )
    out_specs = (P(("grp", "span"), None), P(("grp", "span"), None))
    return jax.shard_map(
        functools.partial(body, grp // n_z, n_z, span // 2),
        mesh=mesh, in_specs=in_specs, out_specs=out_specs, check_vma=False,
    )
```

```python
import functools

import jax
import jax.numpy as jnp
from jax import lax
from jax.experimental import pallas as pl
from jax.experimental.pallas import tpu as pltpu
from jax.sharding import PartitionSpec as P

MESH = pl.DeviceIdType.MESH
F32 = jnp.float32
LANES = 128
ROWS = 8
PIECES = 2


def one_minus_exp(x):
    series = x * (1 - x / 2 * (1 - x / 3 * (1 - x / 4 * (1 - x / 5 * (1 - x / 6)))))
    return jnp.where(x < 0.1, series, 1.0 - jnp.exp(-x))


def kernel(
    n_y, n_z, n_x,
    slopes_hbm, recon_ref, inter_ref, valid_ref, open_ref, closed_ref,
    smooth_hbm, resid_hbm,
    slopes_ref, smooth_ref, resid_ref,
    rbuf, ibuf, modal, state0, back_in, fwd_in, cst, rates, carry,
    a1, a2, a3, b1, b2, b3,
    own_sem, out_sem, r_send, r_recv, i_send, i_recv, e_send, e_recv,
):
    frames = slopes_ref.shape[0]
    modes = recon_ref.shape[1]
    tiles = modes // LANES
    blocks = frames // ROWS
    grp = lax.axis_index("grp")
    span = lax.axis_index("span")
    y, z = grp // n_z, grp % n_z
    x, core = span // 2, span % 2
    n_span = 2 * n_x
    other = x * 2 + (1 - core)
    right = ((x + 1) % n_x) * 2 + core
    left = ((x + n_x - 1) % n_x) * 2 + core

    def far_first(count):
        return sorted(range(1, count), key=lambda k: -min(k, count - k))

    span_peers = [(k, {"span": (span + k) % n_span}) for k in far_first(n_span)]
    z_peers = [(k, {"grp": y * n_z + (z + k) % n_z}) for k in far_first(n_z)]
    y_peers = [(k, {"grp": ((y + k) % n_y) * n_z + z}) for k in far_first(n_y)]

    barrier = pltpu.get_barrier_semaphore()
    everyone = y_peers + z_peers + span_peers
    for _, peer in everyone:
        pl.semaphore_signal(barrier, inc=1, device_id=peer, device_id_type=MESH)

    half_r, half_i = recon_ref.shape[0] // 2, inter_ref.shape[0] // 2

    def r_slot(j, c, h):
        if h is None:
            return rbuf.at[j, c]
        return rbuf.at[j, c, pl.ds(h * half_r, half_r), :]

    def r_own(h):
        return recon_ref if h is None else recon_ref.at[pl.ds(h * half_r, half_r), :]

    def i_slot(j, c, h):
        cols = pl.ds(pl.multiple_of(c * LANES, LANES), LANES)
        if h is None:
            return ibuf.at[j, :, cols]
        return ibuf.at[j, pl.ds(h * half_i, half_i), cols]

    def i_own(h):
        return inter_ref if h is None else inter_ref.at[pl.ds(h * half_i, half_i), :]

    class Gather:
        def __init__(self, slot, own, send, recv):
            self.slot, self.own, self.send, self.recv = slot, own, send, recv
            self.started = []

        def push(self, n, src, dst, to):
            copy = pltpu.make_async_remote_copy(
                src_ref=src, dst_ref=dst, send_sem=self.send.at[n], recv_sem=self.recv.at[n],
                device_id={"span": to}, device_id_type=MESH,
            )
            copy.start()
            self.started.append(copy)

        def arrived(self, n, where):
            pltpu.make_async_remote_copy(
                src_ref=where, dst_ref=where, send_sem=self.send.at[n], recv_sem=self.recv.at[n],
                device_id={"span": other}, device_id_type=MESH,
            ).wait_recv()

        def begin_first(self):
            slot, own = self.slot, self.own
            self.push(0, own(0), slot(3, core, 0), right)
            self.push(2, own(1), slot(1, core, 1), left)

        def begin_second(self):
            slot, own = self.slot, self.own
            self.push(1, own(1), slot(3, core, 1), right)
            self.push(3, own(0), slot(1, core, 0), left)
            self.push(6, own(None), slot(0, core, None), other)

        def relay_first(self):
            slot = self.slot
            self.arrived(0, slot(3, core, 0))
            self.push(4, slot(3, core, 0), slot(2, core, 0), right)
            self.push(7, slot(3, core, 0), slot(3, core, 0), other)
            self.arrived(2, slot(1, core, 1))
            self.push(5, slot(1, core, 1), slot(2, core, 1), left)
            self.push(9, slot(1, core, 1), slot(1, core, 1), other)

        def relay_second(self):
            slot = self.slot
            self.arrived(1, slot(3, core, 1))
            self.push(8, slot(3, core, 1), slot(3, core, 1), other)
            self.arrived(3, slot(1, core, 0))
            self.push(10, slot(1, core, 0), slot(1, core, 0), other)

        def relay_third(self):
            slot = self.slot
            self.arrived(4, slot(2, core, 0))
            self.push(11, slot(2, core, 0), slot(2, core, 0), other)
            self.arrived(5, slot(2, core, 1))
            self.push(12, slot(2, core, 1), slot(2, core, 1), other)

        def wait_chip(self, j):
            there, slot = 1 - core, self.slot
            for n, h in {0: [(6, None)], 3: [(7, 0), (8, 1)], 1: [(9, 1), (10, 0)],
                         2: [(11, 0), (12, 1)]}[j]:
                self.arrived(n, slot(j, there, h))

        def drain(self):
            for copy in self.started:
                copy.wait_send()

    recon = Gather(r_slot, r_own, r_send, r_recv)
    inter = Gather(i_slot, i_own, i_send, i_recv)
    keep_r = pltpu.make_async_copy(recon_ref, r_slot(0, core, None), own_sem.at[0])
    keep_i = pltpu.make_async_copy(inter_ref, i_slot(0, core, None), own_sem.at[1])
    keep_s = pltpu.make_async_copy(slopes_hbm, slopes_ref, own_sem.at[2])

    pl.semaphore_wait(barrier, len(everyone))
    recon.begin_first()
    recon.begin_second()
    keep_r.start()
    keep_s.start()
    keep_i.start()

    row = lax.broadcasted_iota(jnp.int32, (ROWS, LANES), 0)
    rowf = row.astype(F32)
    flag = jnp.broadcast_to(valid_ref[...].astype(F32), (ROWS, LANES))

    def lane(l):
        return pl.ds(l * LANES, LANES)

    def back_scan(source, target, l):
        q1, q2, q4, qw, k8 = (cst[l, n] for n in range(5, 10))
        blend = cst[l, 11]
        parts = []
        for k in range(blocks):
            v = blend * source(k)
            v = v + q1 * pltpu.roll(v, ROWS - 1, 0)
            v = v + q2 * pltpu.roll(v, ROWS - 2, 0)
            v = v + q4 * pltpu.roll(v, ROWS - 4, 0)
            parts.append(v)
        after = jnp.zeros((ROWS, LANES), F32)
        for k in reversed(range(blocks)):
            target[pl.ds(k * ROWS, ROWS), lane(l)] = parts[k] + qw * after
            after = k8 * after + jnp.broadcast_to(parts[k][0:1], (ROWS, LANES))
        return after[0:1]

    def prepare(l):
        a_rate = jnp.broadcast_to(open_ref[:, lane(l)], (ROWS, LANES))
        c_rate = jnp.broadcast_to(closed_ref[:, lane(l)], (ROWS, LANES))
        rates[pl.ds(l, 1), :] = open_ref[:, lane(l)]
        rates[pl.ds(tiles + l, 1), :] = closed_ref[:, lane(l)]
        rate = jnp.where(flag > 0.5, c_rate, a_rate)
        for n, d in enumerate((1, 2, 4)):
            cst[l, n] = jnp.where(row >= d, jnp.exp(-d * rate), 0.0)
            cst[l, 5 + n] = jnp.where(row < ROWS - d, jnp.exp(-d * c_rate), 0.0)
        pw = jnp.exp(-(rowf + 1.0) * rate)
        cst[l, 3] = pw
        cst[l, 4] = jnp.exp(-float(ROWS) * rate)
        cst[l, 8] = jnp.exp(-(float(ROWS) - rowf) * c_rate)
        cst[l, 9] = jnp.exp(-float(ROWS) * c_rate)
        gain = one_minus_exp(c_rate - a_rate)
        cst[l, 10] = flag * (gain / jnp.sqrt(2.0 * c_rate))
        cst[l, 11] = one_minus_exp(a_rate + c_rate)
        power = cst[l, 8]
        for k in reversed(range(blocks)):
            back_in[pl.ds(k * ROWS, ROWS), lane(l)] = power
            power = power * cst[l, 9]
        powers = [pw]
        for k in range(1, blocks):
            powers.append(powers[-1] * cst[l, 4])
        first = back_scan(lambda k: powers[k], fwd_in, l)
        a1[span, pl.ds(tiles + l, 1), :] = first
        a1[span, pl.ds(l, 1), :] = jnp.exp(-float(frames) * rate[0:1])

    prepare(0)
    prepare(1)
    recon.relay_first()
    for l in range(2, tiles):
        prepare(l)

    closed4 = rates[pl.ds(tiles, tiles), :]
    decay4 = jnp.exp(-rates[pl.ds(0, tiles), :])

    def exchange(buf, me, peers, base):
        for k, peer in peers:
            n = k - 1
            copy = pltpu.make_async_remote_copy(
                src_ref=buf.at[me], dst_ref=buf.at[me],
                send_sem=e_send.at[base + n], recv_sem=e_recv.at[base + n],
                device_id=peer, device_id_type=MESH,
            )
            copy.start()
            sent.append(copy)

    def collect(buf, me, peers, base):
        count = len(peers) + 1
        for k, peer in peers:
            n = k - 1
            slot = buf.at[(me + count - k) % count]
            pltpu.make_async_remote_copy(
                src_ref=slot, dst_ref=slot,
                send_sem=e_send.at[base + n], recv_sem=e_recv.at[base + n],
                device_id=peer, device_id_type=MESH,
            ).wait_recv()

    def pair(buf, k):
        return buf[k, pl.ds(0, tiles), :], buf[k, pl.ds(tiles, tiles), :]

    def put(buf, me, parts):
        for q in range(2):
            buf[me, pl.ds(q * tiles, tiles), :] = parts[q]

    def psi(n):
        return jnp.exp(-float(n) * closed4)

    def total_a(a, count, length):
        thr, resp = pair(a, 0)
        for k in range(1, count):
            thr_k, resp_k = pair(a, k)
            resp = resp + psi(k * length) * resp_k * thr
            thr = thr * thr_k
        return thr, resp

    def total_b(a, b, count, length):
        end, start = pair(b, 0)
        for k in range(1, count):
            (thr_k, resp_k), (end_k, start_k) = pair(a, k), pair(b, k)
            start = start + psi(k * length) * (start_k + resp_k * end)
            end = thr_k * end + end_k
        return end, start

    def affine(a, b, me, count, length):
        thr, end = jnp.ones((tiles, LANES), F32), jnp.zeros((tiles, LANES), F32)
        thr_in, end_in = thr, end
        for k in range(count):
            (thr_k, _), (end_k, _) = pair(a, k), pair(b, k)
            thr_in, end_in = jnp.where(me == k, thr, thr_in), jnp.where(me == k, end, end_in)
            thr, end = jnp.where(k <= me, thr * thr_k, thr), jnp.where(k <= me, thr_k * end + end_k, end)
        step = psi(length)
        resp, start = jnp.zeros((tiles, LANES), F32), jnp.zeros((tiles, LANES), F32)
        far = jnp.ones((tiles, LANES), F32)
        for k in range(count - 1, 0, -1):
            (thr_k, resp_k), (end_k, start_k) = pair(a, k), pair(b, k)
            start = jnp.where(k > me, start_k + step * (start + resp * end_k), start)
            resp = jnp.where(k > me, resp_k + step * resp * thr_k, resp)
            far = jnp.where(k > me, far * step, far)
        return thr_in, end_in, far, resp * thr, resp * end + start

    def apply(form, before, after):
        thr_in, end_in, far, resp, start = form
        return thr_in * before + end_in, far * after + resp * before + start

    def solve_top(a, b, me, count, length):
        step = psi(length)
        entering = [jnp.zeros((tiles, LANES), F32)]
        for k in range(count):
            (thr_k, _), (end_k, _) = pair(a, k), pair(b, k)
            entering.append(thr_k * entering[k] + end_k)
        state = decay4 * entering[count]
        mine_in, mine_after = entering[0], state
        for k in range(1, count):
            mine_in = jnp.where(me == k, entering[k], mine_in)
        for k in range(count - 1, 0, -1):
            (_, resp_k), (_, start_k) = pair(a, k), pair(b, k)
            state = step * state + resp_k * entering[k] + start_k
            mine_after = jnp.where(me == k - 1, state, mine_after)
        return mine_in, mine_after

    sent = []
    base_z = n_span - 1
    base_y = base_z + n_z - 1
    late = base_y + n_y - 1
    len_z, len_y = n_span * frames, n_z * n_span * frames
    exchange(a1, span, span_peers, 0)

    def modal_part(j):
        cols = pl.ds(pl.multiple_of(((x + j) % n_x) * 2 * LANES, 2 * LANES), 2 * LANES)
        return jnp.dot(
            slopes_ref[:, cols], rbuf[j].reshape(2 * LANES, modes), preferred_element_type=F32
        )

    recon.relay_second()
    keep_r.wait()
    keep_s.wait()
    recon.wait_chip(0)
    modal[...] = modal_part(0)
    recon.relay_third()
    inter.begin_first()
    recon.wait_chip(3)
    modal[...] += modal_part(3)
    recon.wait_chip(1)
    modal[...] += modal_part(1)
    recon.wait_chip(2)
    modal[...] += modal_part(2)
    collect(a1, span, span_peers, 0)
    put(a2, z, total_a(a1, n_span, frames))
    exchange(a2, z, z_peers, base_z)

    for l in range(tiles):
        p1, p2, p4, pw, f8 = (cst[l, n] for n in range(5))
        inject = cst[l, 10]
        parts = []
        for k in range(blocks):
            v = inject * modal[pl.ds(k * ROWS, ROWS), lane(l)]
            v = v + p1 * pltpu.roll(v, 1, 0)
            v = v + p2 * pltpu.roll(v, 2, 0)
            v = v + p4 * pltpu.roll(v, 4, 0)
            parts.append(v)
        before = jnp.zeros((ROWS, LANES), F32)
        filtered = []
        for k in range(blocks):
            filtered.append(parts[k] + pw * before)
            before = f8 * before + jnp.broadcast_to(parts[k][ROWS - 1:], (ROWS, LANES))
        first = back_scan(lambda k: filtered[k], state0, l)
        b1[span, pl.ds(l, 1), :] = before[0:1]
        b1[span, pl.ds(tiles + l, 1), :] = first

    exchange(b1, span, span_peers, late)
    inter.begin_second()
    inter.relay_first()
    collect(b1, span, span_peers, late)
    put(b2, z, total_b(a1, b1, n_span, frames))
    exchange(b2, z, z_peers, late + base_z)
    collect(a2, z, z_peers, base_z)
    put(a3, y, total_a(a2, n_z, len_z))
    exchange(a3, y, y_peers, base_y)
    inter.relay_second()
    form_x = affine(a1, b1, span, n_span, frames)
    collect(b2, z, z_peers, late + base_z)
    put(b3, y, total_b(a2, b2, n_z, len_z))
    exchange(b3, y, y_peers, late + base_y)
    inter.relay_third()
    form_z = affine(a2, b2, z, n_z, len_z)
    collect(a3, y, y_peers, base_y)
    collect(b3, y, y_peers, late + base_y)

    before, after = solve_top(a3, b3, y, n_y, len_y)
    before, after = apply(form_z, before, after)
    before, after = apply(form_x, before, after)
    carry[pl.ds(0, tiles), :] = before
    carry[pl.ds(tiles, tiles), :] = after
    for l in range(tiles):
        state = (
            state0[:, lane(l)]
            + back_in[:, lane(l)] * carry[pl.ds(tiles + l, 1), :]
            + fwd_in[:, lane(l)] * carry[pl.ds(l, 1), :]
        )
        smooth_ref[:, lane(l)] = state.astype(jnp.bfloat16)
    outs = [pltpu.make_async_copy(smooth_ref, smooth_hbm, out_sem.at[0])]
    outs[0].start()

    keep_i.wait()
    for j in (0, 3, 1, 2):
        inter.wait_chip(j)
        cols = pl.ds(pl.multiple_of(((x + j) % n_x) * 2 * LANES, 2 * LANES), 2 * LANES)
        fitted = jnp.dot(smooth_ref[...], ibuf[j], preferred_element_type=F32)
        resid_ref[:, cols] = (slopes_ref[:, cols].astype(F32) - fitted).astype(jnp.bfloat16)
        outs.append(
            pltpu.make_async_copy(resid_ref.at[:, cols], resid_hbm.at[:, cols], out_sem.at[1 + j])
        )
        outs[-1].start()

    recon.drain()
    inter.drain()
    for copy in sent:
        copy.wait_send()
    for copy in outs:
        copy.wait()


def hand_over(smooth_in, resid_in, smooth_out, resid_out, smooth_buf, resid_buf, in_sem, out_sem):
    arrays = ((smooth_in, smooth_buf, smooth_out), (resid_in, resid_buf, resid_out))
    rows = smooth_in.shape[0] // PIECES
    loads, stores = [], []
    for n, (src, buf, dst) in enumerate(arrays):
        for p in range(PIECES):
            part = pl.ds(p * rows, rows)
            loads.append(pltpu.make_async_copy(src.at[part], buf.at[part], in_sem.at[n, p]))
            stores.append(pltpu.make_async_copy(buf.at[part], dst.at[part], out_sem.at[n, p]))
    for load in loads:
        load.start()
    for load, store in zip(loads, stores):
        load.wait()
        store.start()
    for store in stores:
        store.wait()


def body(n_y, n_z, n_x, slopes, reconstructor, interaction, frame_valid, open_rate, closed_rate):
    frames, n_slopes = slopes.shape
    modes = reconstructor.shape[1]
    tiles = modes // LANES
    n_span = 2 * n_x
    messages = 2 * (n_span - 1 + n_z - 1 + n_y - 1)
    hbm = pl.BlockSpec(memory_space=pl.ANY)
    vmem = pl.BlockSpec(memory_space=pltpu.VMEM)
    whole = (frames, modes)
    smoothed, residual = pl.pallas_call(
        functools.partial(kernel, n_y, n_z, n_x),
        out_shape=(
            jax.ShapeDtypeStruct((frames, modes), jnp.bfloat16),
            jax.ShapeDtypeStruct((frames, n_slopes), jnp.bfloat16),
        ),
        in_specs=[hbm, hbm, hbm, vmem, vmem, vmem],
        out_specs=(hbm, hbm),
        scratch_shapes=[
            pltpu.VMEM((frames, n_slopes), jnp.bfloat16),
            pltpu.VMEM(whole, jnp.bfloat16),
            pltpu.VMEM((frames, n_slopes), jnp.bfloat16),
            pltpu.VMEM((n_x, 2, LANES, modes), jnp.bfloat16),
            pltpu.VMEM((n_x, modes, 2 * LANES), jnp.bfloat16),
            pltpu.VMEM(whole, F32),
            pltpu.VMEM(whole, F32),
            pltpu.VMEM(whole, F32),
            pltpu.VMEM(whole, F32),
            pltpu.VMEM((tiles, 12, ROWS, LANES), F32),
            pltpu.VMEM((2 * tiles, LANES), F32),
            pltpu.VMEM((2 * tiles, LANES), F32),
            *[pltpu.VMEM((n, 2 * tiles, LANES), F32) for n in (n_span, n_z, n_y) * 2],
            pltpu.SemaphoreType.DMA((3,)),
            pltpu.SemaphoreType.DMA((1 + n_x,)),
            pltpu.SemaphoreType.DMA((13,)),
            pltpu.SemaphoreType.DMA((13,)),
            pltpu.SemaphoreType.DMA((13,)),
            pltpu.SemaphoreType.DMA((13,)),
            pltpu.SemaphoreType.DMA((messages,)),
            pltpu.SemaphoreType.DMA((messages,)),
        ],
        compiler_params=pltpu.CompilerParams(collective_id=0, has_side_effects=True),
    )(
        slopes, reconstructor, interaction, frame_valid.reshape(1, 1),
        open_rate.reshape(1, modes), closed_rate.reshape(1, modes),
    )
    return pl.pallas_call(
        hand_over,
        out_shape=(
            jax.ShapeDtypeStruct((frames, modes), jnp.bfloat16),
            jax.ShapeDtypeStruct((frames, n_slopes), jnp.bfloat16),
        ),
        in_specs=[hbm, hbm],
        out_specs=(hbm, hbm),
        scratch_shapes=[
            pltpu.VMEM((frames, modes), jnp.bfloat16),
            pltpu.VMEM((frames, n_slopes), jnp.bfloat16),
            pltpu.SemaphoreType.DMA((2, PIECES)),
            pltpu.SemaphoreType.DMA((2, PIECES)),
        ],
    )(smoothed, residual)


def solution(mesh):
    grp, span = mesh.shape["grp"], mesh.shape["span"]
    n_z = 8 if grp % 8 == 0 else 1
    in_specs = (
        P(("grp", "span"), None),
        P("span", None),
        P(None, "span"),
        P(("grp", "span")),
        P(),
        P(),
    )
    out_specs = (P(("grp", "span"), None), P(("grp", "span"), None))
    return jax.shard_map(
        functools.partial(body, grp // n_z, n_z, span // 2),
        mesh=mesh, in_specs=in_specs, out_specs=out_specs, check_vma=False,
    )
```

```python
import functools

import jax
import jax.numpy as jnp
from jax import lax
from jax.experimental import pallas as pl
from jax.experimental.pallas import tpu as pltpu
from jax.sharding import PartitionSpec as P

MESH = pl.DeviceIdType.MESH
F32 = jnp.float32
LANES = 128
ROWS = 8


def one_minus_exp(x):
    series = x * (1 - x / 2 * (1 - x / 3 * (1 - x / 4 * (1 - x / 5 * (1 - x / 6)))))
    return jnp.where(x < 0.1, series, 1.0 - jnp.exp(-x))


def kernel(
    n_y, n_z, n_x,
    slopes_hbm, recon_ref, inter_ref, valid_ref, open_hbm, closed_hbm,
    smooth_hbm, resid_hbm,
    open_ref, closed_ref, slopes_ref, smooth_ref, resid_ref,
    rbuf, ibuf, modal, state0, back_in, fwd_in, cst, rates, carry,
    a1, a2, a3, b1, b2, b3,
    own_sem, out_sem, r_send, r_recv, i_send, i_recv, e_send, e_recv,
):
    frames = slopes_ref.shape[0]
    modes = recon_ref.shape[1]
    tiles = modes // LANES
    blocks = frames // ROWS
    grp = lax.axis_index("grp")
    span = lax.axis_index("span")
    y, z = grp // n_z, grp % n_z
    x, core = span // 2, span % 2
    n_span = 2 * n_x
    other = x * 2 + (1 - core)
    right = ((x + 1) % n_x) * 2 + core
    left = ((x + n_x - 1) % n_x) * 2 + core

    def far_first(count):
        return sorted(range(1, count), key=lambda k: -min(k, count - k))

    span_peers = [(k, {"span": (span + k) % n_span}) for k in far_first(n_span)]
    z_peers = [(k, {"grp": y * n_z + (z + k) % n_z}) for k in far_first(n_z)]
    y_peers = [(k, {"grp": ((y + k) % n_y) * n_z + z}) for k in far_first(n_y)]

    barrier = pltpu.get_barrier_semaphore()
    everyone = y_peers + z_peers + span_peers
    for _, peer in everyone:
        pl.semaphore_signal(barrier, inc=1, device_id=peer, device_id_type=MESH)

    half_r, half_i = recon_ref.shape[0] // 2, inter_ref.shape[0] // 2

    def r_slot(j, c, h):
        if h is None:
            return rbuf.at[j, c]
        return rbuf.at[j, c, pl.ds(h * half_r, half_r), :]

    def r_own(h):
        return recon_ref if h is None else recon_ref.at[pl.ds(h * half_r, half_r), :]

    def i_slot(j, c, h):
        cols = pl.ds(pl.multiple_of(c * LANES, LANES), LANES)
        if h is None:
            return ibuf.at[j, :, cols]
        return ibuf.at[j, pl.ds(h * half_i, half_i), cols]

    def i_own(h):
        return inter_ref if h is None else inter_ref.at[pl.ds(h * half_i, half_i), :]

    class Gather:
        def __init__(self, slot, own, send, recv):
            self.slot, self.own, self.send, self.recv = slot, own, send, recv
            self.started = []

        def push(self, n, src, dst, to):
            copy = pltpu.make_async_remote_copy(
                src_ref=src, dst_ref=dst, send_sem=self.send.at[n], recv_sem=self.recv.at[n],
                device_id={"span": to}, device_id_type=MESH,
            )
            copy.start()
            self.started.append(copy)

        def arrived(self, n, where):
            pltpu.make_async_remote_copy(
                src_ref=where, dst_ref=where, send_sem=self.send.at[n], recv_sem=self.recv.at[n],
                device_id={"span": other}, device_id_type=MESH,
            ).wait_recv()

        def begin_first(self):
            slot, own = self.slot, self.own
            self.push(0, own(0), slot(3, core, 0), right)
            self.push(2, own(1), slot(1, core, 1), left)

        def begin_second(self):
            slot, own = self.slot, self.own
            self.push(1, own(1), slot(3, core, 1), right)
            self.push(3, own(0), slot(1, core, 0), left)
            self.push(6, own(None), slot(0, core, None), other)

        def relay_first(self):
            slot = self.slot
            self.arrived(0, slot(3, core, 0))
            self.push(4, slot(3, core, 0), slot(2, core, 0), right)
            self.push(7, slot(3, core, 0), slot(3, core, 0), other)
            self.arrived(2, slot(1, core, 1))
            self.push(5, slot(1, core, 1), slot(2, core, 1), left)
            self.push(9, slot(1, core, 1), slot(1, core, 1), other)

        def relay_second(self):
            slot = self.slot
            self.arrived(1, slot(3, core, 1))
            self.push(8, slot(3, core, 1), slot(3, core, 1), other)
            self.arrived(3, slot(1, core, 0))
            self.push(10, slot(1, core, 0), slot(1, core, 0), other)

        def relay_third(self):
            slot = self.slot
            self.arrived(4, slot(2, core, 0))
            self.push(11, slot(2, core, 0), slot(2, core, 0), other)
            self.arrived(5, slot(2, core, 1))
            self.push(12, slot(2, core, 1), slot(2, core, 1), other)

        def wait_chip(self, j):
            there, slot = 1 - core, self.slot
            for n, h in {0: [(6, None)], 3: [(7, 0), (8, 1)], 1: [(9, 1), (10, 0)],
                         2: [(11, 0), (12, 1)]}[j]:
                self.arrived(n, slot(j, there, h))

        def drain(self):
            for copy in self.started:
                copy.wait_send()

    recon = Gather(r_slot, r_own, r_send, r_recv)
    inter = Gather(i_slot, i_own, i_send, i_recv)
    keep_r = pltpu.make_async_copy(recon_ref, r_slot(0, core, None), own_sem.at[0])
    keep_i = pltpu.make_async_copy(inter_ref, i_slot(0, core, None), own_sem.at[1])
    keep_o = pltpu.make_async_copy(open_hbm, open_ref, own_sem.at[3])
    keep_c = pltpu.make_async_copy(closed_hbm, closed_ref, own_sem.at[4])
    keep_o.start()
    keep_c.start()
    keep_s = pltpu.make_async_copy(slopes_hbm, slopes_ref, own_sem.at[2])

    pl.semaphore_wait(barrier, len(everyone))
    recon.begin_first()
    recon.begin_second()
    keep_r.start()
    keep_s.start()
    keep_i.start()

    row = lax.broadcasted_iota(jnp.int32, (ROWS, LANES), 0)
    rowf = row.astype(F32)
    flag = jnp.broadcast_to(valid_ref[...].astype(F32), (ROWS, LANES))

    def lane(l):
        return pl.ds(l * LANES, LANES)

    def back_scan(source, target, l):
        q1, q2, q4, qw, k8 = (cst[l, n] for n in range(5, 10))
        blend = cst[l, 11]
        parts = []
        for k in range(blocks):
            v = blend * source(k)
            v = v + q1 * pltpu.roll(v, ROWS - 1, 0)
            v = v + q2 * pltpu.roll(v, ROWS - 2, 0)
            v = v + q4 * pltpu.roll(v, ROWS - 4, 0)
            parts.append(v)
        after = jnp.zeros((ROWS, LANES), F32)
        for k in reversed(range(blocks)):
            target[pl.ds(k * ROWS, ROWS), lane(l)] = parts[k] + qw * after
            after = k8 * after + jnp.broadcast_to(parts[k][0:1], (ROWS, LANES))
        return after[0:1]

    def prepare(l):
        a_rate = jnp.broadcast_to(open_ref[:, lane(l)], (ROWS, LANES))
        c_rate = jnp.broadcast_to(closed_ref[:, lane(l)], (ROWS, LANES))
        rates[pl.ds(l, 1), :] = open_ref[:, lane(l)]
        rates[pl.ds(tiles + l, 1), :] = closed_ref[:, lane(l)]
        rate = jnp.where(flag > 0.5, c_rate, a_rate)
        for n, d in enumerate((1, 2, 4)):
            cst[l, n] = jnp.where(row >= d, jnp.exp(-d * rate), 0.0)
            cst[l, 5 + n] = jnp.where(row < ROWS - d, jnp.exp(-d * c_rate), 0.0)
        pw = jnp.exp(-(rowf + 1.0) * rate)
        cst[l, 3] = pw
        cst[l, 4] = jnp.exp(-float(ROWS) * rate)
        cst[l, 8] = jnp.exp(-(float(ROWS) - rowf) * c_rate)
        cst[l, 9] = jnp.exp(-float(ROWS) * c_rate)
        gain = one_minus_exp(c_rate - a_rate)
        cst[l, 10] = flag * (gain / jnp.sqrt(2.0 * c_rate))
        cst[l, 11] = one_minus_exp(a_rate + c_rate)
        power = cst[l, 8]
        for k in reversed(range(blocks)):
            back_in[pl.ds(k * ROWS, ROWS), lane(l)] = power
            power = power * cst[l, 9]
        powers = [pw]
        for k in range(1, blocks):
            powers.append(powers[-1] * cst[l, 4])
        first = back_scan(lambda k: powers[k], fwd_in, l)
        a1[span, pl.ds(tiles + l, 1), :] = first
        a1[span, pl.ds(l, 1), :] = jnp.exp(-float(frames) * rate[0:1])

    keep_o.wait()
    keep_c.wait()
    prepare(0)
    prepare(1)
    recon.relay_first()
    for l in range(2, tiles):
        prepare(l)

    closed4 = rates[pl.ds(tiles, tiles), :]
    decay4 = jnp.exp(-rates[pl.ds(0, tiles), :])

    def exchange(buf, me, peers, base):
        for k, peer in peers:
            n = k - 1
            copy = pltpu.make_async_remote_copy(
                src_ref=buf.at[me], dst_ref=buf.at[me],
                send_sem=e_send.at[base + n], recv_sem=e_recv.at[base + n],
                device_id=peer, device_id_type=MESH,
            )
            copy.start()
            sent.append(copy)

    def collect(buf, me, peers, base):
        count = len(peers) + 1
        for k, peer in peers:
            n = k - 1
            slot = buf.at[(me + count - k) % count]
            pltpu.make_async_remote_copy(
                src_ref=slot, dst_ref=slot,
                send_sem=e_send.at[base + n], recv_sem=e_recv.at[base + n],
                device_id=peer, device_id_type=MESH,
            ).wait_recv()

    def pair(buf, k):
        return buf[k, pl.ds(0, tiles), :], buf[k, pl.ds(tiles, tiles), :]

    def put(buf, me, parts):
        for q in range(2):
            buf[me, pl.ds(q * tiles, tiles), :] = parts[q]

    def psi(n):
        return jnp.exp(-float(n) * closed4)

    def total_a(a, count, length):
        thr, resp = pair(a, 0)
        for k in range(1, count):
            thr_k, resp_k = pair(a, k)
            resp = resp + psi(k * length) * resp_k * thr
            thr = thr * thr_k
        return thr, resp

    def total_b(a, b, count, length):
        end, start = pair(b, 0)
        for k in range(1, count):
            (thr_k, resp_k), (end_k, start_k) = pair(a, k), pair(b, k)
            start = start + psi(k * length) * (start_k + resp_k * end)
            end = thr_k * end + end_k
        return end, start

    def affine(a, b, me, count, length):
        thr, end = jnp.ones((tiles, LANES), F32), jnp.zeros((tiles, LANES), F32)
        thr_in, end_in = thr, end
        for k in range(count):
            (thr_k, _), (end_k, _) = pair(a, k), pair(b, k)
            thr_in, end_in = jnp.where(me == k, thr, thr_in), jnp.where(me == k, end, end_in)
            thr, end = jnp.where(k <= me, thr * thr_k, thr), jnp.where(k <= me, thr_k * end + end_k, end)
        step = psi(length)
        resp, start = jnp.zeros((tiles, LANES), F32), jnp.zeros((tiles, LANES), F32)
        far = jnp.ones((tiles, LANES), F32)
        for k in range(count - 1, 0, -1):
            (thr_k, resp_k), (end_k, start_k) = pair(a, k), pair(b, k)
            start = jnp.where(k > me, start_k + step * (start + resp * end_k), start)
            resp = jnp.where(k > me, resp_k + step * resp * thr_k, resp)
            far = jnp.where(k > me, far * step, far)
        return thr_in, end_in, far, resp * thr, resp * end + start

    def apply(form, before, after):
        thr_in, end_in, far, resp, start = form
        return thr_in * before + end_in, far * after + resp * before + start

    def solve_top(a, b, me, count, length):
        step = psi(length)
        entering = [jnp.zeros((tiles, LANES), F32)]
        for k in range(count):
            (thr_k, _), (end_k, _) = pair(a, k), pair(b, k)
            entering.append(thr_k * entering[k] + end_k)
        state = decay4 * entering[count]
        mine_in, mine_after = entering[0], state
        for k in range(1, count):
            mine_in = jnp.where(me == k, entering[k], mine_in)
        for k in range(count - 1, 0, -1):
            (_, resp_k), (_, start_k) = pair(a, k), pair(b, k)
            state = step * state + resp_k * entering[k] + start_k
            mine_after = jnp.where(me == k - 1, state, mine_after)
        return mine_in, mine_after

    sent = []
    base_z = n_span - 1
    base_y = base_z + n_z - 1
    late = base_y + n_y - 1
    len_z, len_y = n_span * frames, n_z * n_span * frames
    exchange(a1, span, span_peers, 0)

    def modal_part(j):
        cols = pl.ds(pl.multiple_of(((x + j) % n_x) * 2 * LANES, 2 * LANES), 2 * LANES)
        return jnp.dot(
            slopes_ref[:, cols], rbuf[j].reshape(2 * LANES, modes), preferred_element_type=F32
        )

    recon.relay_second()
    keep_r.wait()
    keep_s.wait()
    recon.wait_chip(0)
    modal[...] = modal_part(0)
    recon.relay_third()
    inter.begin_first()
    recon.wait_chip(3)
    modal[...] += modal_part(3)
    recon.wait_chip(1)
    modal[...] += modal_part(1)
    recon.wait_chip(2)
    modal[...] += modal_part(2)
    collect(a1, span, span_peers, 0)
    put(a2, z, total_a(a1, n_span, frames))
    exchange(a2, z, z_peers, base_z)

    for l in range(tiles):
        p1, p2, p4, pw, f8 = (cst[l, n] for n in range(5))
        inject = cst[l, 10]
        parts = []
        for k in range(blocks):
            v = inject * modal[pl.ds(k * ROWS, ROWS), lane(l)]
            v = v + p1 * pltpu.roll(v, 1, 0)
            v = v + p2 * pltpu.roll(v, 2, 0)
            v = v + p4 * pltpu.roll(v, 4, 0)
            parts.append(v)
        before = jnp.zeros((ROWS, LANES), F32)
        filtered = []
        for k in range(blocks):
            filtered.append(parts[k] + pw * before)
            before = f8 * before + jnp.broadcast_to(parts[k][ROWS - 1:], (ROWS, LANES))
        first = back_scan(lambda k: filtered[k], state0, l)
        b1[span, pl.ds(l, 1), :] = before[0:1]
        b1[span, pl.ds(tiles + l, 1), :] = first

    exchange(b1, span, span_peers, late)
    inter.begin_second()
    inter.relay_first()
    collect(b1, span, span_peers, late)
    put(b2, z, total_b(a1, b1, n_span, frames))
    exchange(b2, z, z_peers, late + base_z)
    collect(a2, z, z_peers, base_z)
    put(a3, y, total_a(a2, n_z, len_z))
    exchange(a3, y, y_peers, base_y)
    inter.relay_second()
    form_x = affine(a1, b1, span, n_span, frames)
    collect(b2, z, z_peers, late + base_z)
    put(b3, y, total_b(a2, b2, n_z, len_z))
    exchange(b3, y, y_peers, late + base_y)
    inter.relay_third()
    form_z = affine(a2, b2, z, n_z, len_z)
    collect(a3, y, y_peers, base_y)
    collect(b3, y, y_peers, late + base_y)

    before, after = solve_top(a3, b3, y, n_y, len_y)
    before, after = apply(form_z, before, after)
    before, after = apply(form_x, before, after)
    carry[pl.ds(0, tiles), :] = before
    carry[pl.ds(tiles, tiles), :] = after
    for l in range(tiles):
        state = (
            state0[:, lane(l)]
            + back_in[:, lane(l)] * carry[pl.ds(tiles + l, 1), :]
            + fwd_in[:, lane(l)] * carry[pl.ds(l, 1), :]
        )
        smooth_ref[:, lane(l)] = state.astype(jnp.bfloat16)
    outs = [pltpu.make_async_copy(smooth_ref, smooth_hbm, out_sem.at[0])]
    outs[0].start()

    keep_i.wait()
    for j in (0, 3, 1, 2):
        inter.wait_chip(j)
        cols = pl.ds(pl.multiple_of(((x + j) % n_x) * 2 * LANES, 2 * LANES), 2 * LANES)
        fitted = jnp.dot(smooth_ref[...], ibuf[j], preferred_element_type=F32)
        resid_ref[:, cols] = (slopes_ref[:, cols].astype(F32) - fitted).astype(jnp.bfloat16)
        outs.append(
            pltpu.make_async_copy(resid_ref.at[:, cols], resid_hbm.at[:, cols], out_sem.at[1 + j])
        )
        outs[-1].start()

    recon.drain()
    inter.drain()
    for copy in sent:
        copy.wait_send()
    for copy in outs:
        copy.wait()


def hand_over(smooth_in, resid_in, smooth_out, resid_out, sems):
    stores = (
        pltpu.make_async_copy(resid_in, resid_out, sems.at[0]),
        pltpu.make_async_copy(smooth_in, smooth_out, sems.at[1]),
    )
    for store in stores:
        store.start()
    for store in stores:
        store.wait()


def body(n_y, n_z, n_x, slopes, reconstructor, interaction, frame_valid, open_rate, closed_rate):
    frames, n_slopes = slopes.shape
    modes = reconstructor.shape[1]
    tiles = modes // LANES
    n_span = 2 * n_x
    messages = 2 * (n_span - 1 + n_z - 1 + n_y - 1)
    hbm = pl.BlockSpec(memory_space=pl.ANY)
    vmem = pl.BlockSpec(memory_space=pltpu.VMEM)
    far = pl.BlockSpec(memory_space=pltpu.HBM)
    whole = (frames, modes)
    pinned = [
        pltpu.with_memory_space_constraint(v, pltpu.HBM)
        for v in (
            slopes, reconstructor, interaction,
            open_rate.reshape(1, modes), closed_rate.reshape(1, modes),
        )
    ]
    smoothed, residual = pl.pallas_call(
        functools.partial(kernel, n_y, n_z, n_x),
        out_shape=(
            jax.ShapeDtypeStruct((frames, modes), jnp.bfloat16),
            jax.ShapeDtypeStruct((frames, n_slopes), jnp.bfloat16),
        ),
        in_specs=[far, far, far, vmem, far, far],
        out_specs=(hbm, hbm),
        scratch_shapes=[
            pltpu.VMEM((1, modes), F32),
            pltpu.VMEM((1, modes), F32),
            pltpu.VMEM((frames, n_slopes), jnp.bfloat16),
            pltpu.VMEM(whole, jnp.bfloat16),
            pltpu.VMEM((frames, n_slopes), jnp.bfloat16),
            pltpu.VMEM((n_x, 2, LANES, modes), jnp.bfloat16),
            pltpu.VMEM((n_x, modes, 2 * LANES), jnp.bfloat16),
            pltpu.VMEM(whole, F32),
            pltpu.VMEM(whole, F32),
            pltpu.VMEM(whole, F32),
            pltpu.VMEM(whole, F32),
            pltpu.VMEM((tiles, 12, ROWS, LANES), F32),
            pltpu.VMEM((2 * tiles, LANES), F32),
            pltpu.VMEM((2 * tiles, LANES), F32),
            *[pltpu.VMEM((n, 2 * tiles, LANES), F32) for n in (n_span, n_z, n_y) * 2],
            pltpu.SemaphoreType.DMA((5,)),
            pltpu.SemaphoreType.DMA((1 + n_x,)),
            pltpu.SemaphoreType.DMA((13,)),
            pltpu.SemaphoreType.DMA((13,)),
            pltpu.SemaphoreType.DMA((13,)),
            pltpu.SemaphoreType.DMA((13,)),
            pltpu.SemaphoreType.DMA((messages,)),
            pltpu.SemaphoreType.DMA((messages,)),
        ],
        compiler_params=pltpu.CompilerParams(
            collective_id=0, has_side_effects=True, vmem_limit_bytes=16 << 20
        ),
    )(
        *pinned[:3],
        frame_valid.reshape(1, 1),
        *pinned[3:],
    )
    return pl.pallas_call(
        hand_over,
        out_shape=(
            jax.ShapeDtypeStruct((frames, modes), jnp.bfloat16),
            jax.ShapeDtypeStruct((frames, n_slopes), jnp.bfloat16),
        ),
        in_specs=[hbm, hbm],
        out_specs=(far, far),
        scratch_shapes=[pltpu.SemaphoreType.DMA((2,))],
        compiler_params=pltpu.CompilerParams(vmem_limit_bytes=8 << 20),
    )(smoothed, residual)


def solution(mesh):
    grp, span = mesh.shape["grp"], mesh.shape["span"]
    n_z = 8 if grp % 8 == 0 else 1
    in_specs = (
        P(("grp", "span"), None),
        P("span", None),
        P(None, "span"),
        P(("grp", "span")),
        P(),
        P(),
    )
    out_specs = (P(("grp", "span"), None), P(("grp", "span"), None))
    return jax.shard_map(
        functools.partial(body, grp // n_z, n_z, span // 2),
        mesh=mesh, in_specs=in_specs, out_specs=out_specs, check_vma=False,
    )
```

```python
import functools

import jax
import jax.numpy as jnp
from jax import lax
from jax.experimental import pallas as pl
from jax.experimental.pallas import tpu as pltpu
from jax.sharding import PartitionSpec as P

MESH = pl.DeviceIdType.MESH
F32 = jnp.float32
LANES = 128
ROWS = 8


def one_minus_exp(x):
    series = x * (1 - x / 2 * (1 - x / 3 * (1 - x / 4 * (1 - x / 5 * (1 - x / 6)))))
    return jnp.where(x < 0.1, series, 1.0 - jnp.exp(-x))


def kernel(
    n_y, n_z, n_x,
    slopes_hbm, recon_ref, inter_ref, valid_ref, open_hbm, closed_hbm,
    smooth_ref, resid_ref,
    open_ref, closed_ref, slopes_ref,
    rbuf, ibuf, modal, state0, back_in, fwd_in, cst, rates, carry,
    a1, a2, a3, b1, b2, b3,
    own_sem, r_send, r_recv, i_send, i_recv, e_send, e_recv,
):
    frames = slopes_ref.shape[0]
    modes = recon_ref.shape[1]
    tiles = modes // LANES
    blocks = frames // ROWS
    grp = lax.axis_index("grp")
    span = lax.axis_index("span")
    y, z = grp // n_z, grp % n_z
    x, core = span // 2, span % 2
    n_span = 2 * n_x
    other = x * 2 + (1 - core)
    right = ((x + 1) % n_x) * 2 + core
    left = ((x + n_x - 1) % n_x) * 2 + core

    def far_first(count):
        return sorted(range(1, count), key=lambda k: -min(k, count - k))

    span_peers = [(k, {"span": (span + k) % n_span}) for k in far_first(n_span)]
    z_peers = [(k, {"grp": y * n_z + (z + k) % n_z}) for k in far_first(n_z)]
    y_peers = [(k, {"grp": ((y + k) % n_y) * n_z + z}) for k in far_first(n_y)]

    barrier = pltpu.get_barrier_semaphore()
    everyone = y_peers + z_peers + span_peers
    for _, peer in everyone:
        pl.semaphore_signal(barrier, inc=1, device_id=peer, device_id_type=MESH)

    half_r, half_i = recon_ref.shape[0] // 2, inter_ref.shape[0] // 2

    def r_slot(j, c, h):
        if h is None:
            return rbuf.at[j, c]
        return rbuf.at[j, c, pl.ds(h * half_r, half_r), :]

    def r_own(h):
        return recon_ref if h is None else recon_ref.at[pl.ds(h * half_r, half_r), :]

    def i_slot(j, c, h):
        cols = pl.ds(pl.multiple_of(c * LANES, LANES), LANES)
        if h is None:
            return ibuf.at[j, :, cols]
        return ibuf.at[j, pl.ds(h * half_i, half_i), cols]

    def i_own(h):
        return inter_ref if h is None else inter_ref.at[pl.ds(h * half_i, half_i), :]

    class Gather:
        def __init__(self, slot, own, send, recv):
            self.slot, self.own, self.send, self.recv = slot, own, send, recv
            self.started = []

        def push(self, n, src, dst, to):
            copy = pltpu.make_async_remote_copy(
                src_ref=src, dst_ref=dst, send_sem=self.send.at[n], recv_sem=self.recv.at[n],
                device_id={"span": to}, device_id_type=MESH,
            )
            copy.start()
            self.started.append(copy)

        def arrived(self, n, where):
            pltpu.make_async_remote_copy(
                src_ref=where, dst_ref=where, send_sem=self.send.at[n], recv_sem=self.recv.at[n],
                device_id={"span": other}, device_id_type=MESH,
            ).wait_recv()

        def begin_first(self):
            slot, own = self.slot, self.own
            self.push(0, own(0), slot(3, core, 0), right)
            self.push(2, own(1), slot(1, core, 1), left)

        def begin_second(self):
            slot, own = self.slot, self.own
            self.push(1, own(1), slot(3, core, 1), right)
            self.push(3, own(0), slot(1, core, 0), left)
            self.push(6, own(None), slot(0, core, None), other)

        def relay_first(self):
            slot = self.slot
            self.arrived(0, slot(3, core, 0))
            self.push(4, slot(3, core, 0), slot(2, core, 0), right)
            self.push(7, slot(3, core, 0), slot(3, core, 0), other)
            self.arrived(2, slot(1, core, 1))
            self.push(5, slot(1, core, 1), slot(2, core, 1), left)
            self.push(9, slot(1, core, 1), slot(1, core, 1), other)

        def relay_second(self):
            slot = self.slot
            self.arrived(1, slot(3, core, 1))
            self.push(8, slot(3, core, 1), slot(3, core, 1), other)
            self.arrived(3, slot(1, core, 0))
            self.push(10, slot(1, core, 0), slot(1, core, 0), other)

        def relay_third(self):
            slot = self.slot
            self.arrived(4, slot(2, core, 0))
            self.push(11, slot(2, core, 0), slot(2, core, 0), other)
            self.arrived(5, slot(2, core, 1))
            self.push(12, slot(2, core, 1), slot(2, core, 1), other)

        def wait_chip(self, j):
            there, slot = 1 - core, self.slot
            for n, h in {0: [(6, None)], 3: [(7, 0), (8, 1)], 1: [(9, 1), (10, 0)],
                         2: [(11, 0), (12, 1)]}[j]:
                self.arrived(n, slot(j, there, h))

        def drain(self):
            for copy in self.started:
                copy.wait_send()

    recon = Gather(r_slot, r_own, r_send, r_recv)
    inter = Gather(i_slot, i_own, i_send, i_recv)
    keep_r = pltpu.make_async_copy(recon_ref, r_slot(0, core, None), own_sem.at[0])
    keep_i = pltpu.make_async_copy(inter_ref, i_slot(0, core, None), own_sem.at[1])
    keep_o = pltpu.make_async_copy(open_hbm, open_ref, own_sem.at[3])
    keep_c = pltpu.make_async_copy(closed_hbm, closed_ref, own_sem.at[4])
    keep_o.start()
    keep_c.start()
    keep_s = pltpu.make_async_copy(slopes_hbm, slopes_ref, own_sem.at[2])

    pl.semaphore_wait(barrier, len(everyone))
    recon.begin_first()
    recon.begin_second()
    keep_r.start()
    keep_s.start()
    keep_i.start()

    row = lax.broadcasted_iota(jnp.int32, (ROWS, LANES), 0)
    rowf = row.astype(F32)
    flag = jnp.broadcast_to(valid_ref[...].astype(F32), (ROWS, LANES))

    def lane(l):
        return pl.ds(l * LANES, LANES)

    def back_scan(source, target, l):
        q1, q2, q4, qw, k8 = (cst[l, n] for n in range(5, 10))
        blend = cst[l, 11]
        parts = []
        for k in range(blocks):
            v = blend * source(k)
            v = v + q1 * pltpu.roll(v, ROWS - 1, 0)
            v = v + q2 * pltpu.roll(v, ROWS - 2, 0)
            v = v + q4 * pltpu.roll(v, ROWS - 4, 0)
            parts.append(v)
        after = jnp.zeros((ROWS, LANES), F32)
        for k in reversed(range(blocks)):
            target[pl.ds(k * ROWS, ROWS), lane(l)] = parts[k] + qw * after
            after = k8 * after + jnp.broadcast_to(parts[k][0:1], (ROWS, LANES))
        return after[0:1]

    def prepare(l):
        a_rate = jnp.broadcast_to(open_ref[:, lane(l)], (ROWS, LANES))
        c_rate = jnp.broadcast_to(closed_ref[:, lane(l)], (ROWS, LANES))
        rates[pl.ds(l, 1), :] = open_ref[:, lane(l)]
        rates[pl.ds(tiles + l, 1), :] = closed_ref[:, lane(l)]
        rate = jnp.where(flag > 0.5, c_rate, a_rate)
        for n, d in enumerate((1, 2, 4)):
            cst[l, n] = jnp.where(row >= d, jnp.exp(-d * rate), 0.0)
            cst[l, 5 + n] = jnp.where(row < ROWS - d, jnp.exp(-d * c_rate), 0.0)
        pw = jnp.exp(-(rowf + 1.0) * rate)
        cst[l, 3] = pw
        cst[l, 4] = jnp.exp(-float(ROWS) * rate)
        cst[l, 8] = jnp.exp(-(float(ROWS) - rowf) * c_rate)
        cst[l, 9] = jnp.exp(-float(ROWS) * c_rate)
        gain = one_minus_exp(c_rate - a_rate)
        cst[l, 10] = flag * (gain / jnp.sqrt(2.0 * c_rate))
        cst[l, 11] = one_minus_exp(a_rate + c_rate)
        power = cst[l, 8]
        for k in reversed(range(blocks)):
            back_in[pl.ds(k * ROWS, ROWS), lane(l)] = power
            power = power * cst[l, 9]
        powers = [pw]
        for k in range(1, blocks):
            powers.append(powers[-1] * cst[l, 4])
        first = back_scan(lambda k: powers[k], fwd_in, l)
        a1[span, pl.ds(tiles + l, 1), :] = first
        a1[span, pl.ds(l, 1), :] = jnp.exp(-float(frames) * rate[0:1])

    keep_o.wait()
    keep_c.wait()
    prepare(0)
    prepare(1)
    recon.relay_first()
    for l in range(2, tiles):
        prepare(l)

    closed4 = rates[pl.ds(tiles, tiles), :]
    decay4 = jnp.exp(-rates[pl.ds(0, tiles), :])

    def exchange(buf, me, peers, base):
        for k, peer in peers:
            n = k - 1
            copy = pltpu.make_async_remote_copy(
                src_ref=buf.at[me], dst_ref=buf.at[me],
                send_sem=e_send.at[base + n], recv_sem=e_recv.at[base + n],
                device_id=peer, device_id_type=MESH,
            )
            copy.start()
            sent.append(copy)

    def collect(buf, me, peers, base):
        count = len(peers) + 1
        for k, peer in peers:
            n = k - 1
            slot = buf.at[(me + count - k) % count]
            pltpu.make_async_remote_copy(
                src_ref=slot, dst_ref=slot,
                send_sem=e_send.at[base + n], recv_sem=e_recv.at[base + n],
                device_id=peer, device_id_type=MESH,
            ).wait_recv()

    def pair(buf, k):
        return buf[k, pl.ds(0, tiles), :], buf[k, pl.ds(tiles, tiles), :]

    def put(buf, me, parts):
        for q in range(2):
            buf[me, pl.ds(q * tiles, tiles), :] = parts[q]

    def psi(n):
        return jnp.exp(-float(n) * closed4)

    def total_a(a, count, length):
        thr, resp = pair(a, 0)
        for k in range(1, count):
            thr_k, resp_k = pair(a, k)
            resp = resp + psi(k * length) * resp_k * thr
            thr = thr * thr_k
        return thr, resp

    def total_b(a, b, count, length):
        end, start = pair(b, 0)
        for k in range(1, count):
            (thr_k, resp_k), (end_k, start_k) = pair(a, k), pair(b, k)
            start = start + psi(k * length) * (start_k + resp_k * end)
            end = thr_k * end + end_k
        return end, start

    def affine(a, b, me, count, length):
        thr, end = jnp.ones((tiles, LANES), F32), jnp.zeros((tiles, LANES), F32)
        thr_in, end_in = thr, end
        for k in range(count):
            (thr_k, _), (end_k, _) = pair(a, k), pair(b, k)
            thr_in, end_in = jnp.where(me == k, thr, thr_in), jnp.where(me == k, end, end_in)
            thr, end = jnp.where(k <= me, thr * thr_k, thr), jnp.where(k <= me, thr_k * end + end_k, end)
        step = psi(length)
        resp, start = jnp.zeros((tiles, LANES), F32), jnp.zeros((tiles, LANES), F32)
        far = jnp.ones((tiles, LANES), F32)
        for k in range(count - 1, 0, -1):
            (thr_k, resp_k), (end_k, start_k) = pair(a, k), pair(b, k)
            start = jnp.where(k > me, start_k + step * (start + resp * end_k), start)
            resp = jnp.where(k > me, resp_k + step * resp * thr_k, resp)
            far = jnp.where(k > me, far * step, far)
        return thr_in, end_in, far, resp * thr, resp * end + start

    def apply(form, before, after):
        thr_in, end_in, far, resp, start = form
        return thr_in * before + end_in, far * after + resp * before + start

    def solve_top(a, b, me, count, length):
        step = psi(length)
        entering = [jnp.zeros((tiles, LANES), F32)]
        for k in range(count):
            (thr_k, _), (end_k, _) = pair(a, k), pair(b, k)
            entering.append(thr_k * entering[k] + end_k)
        state = decay4 * entering[count]
        mine_in, mine_after = entering[0], state
        for k in range(1, count):
            mine_in = jnp.where(me == k, entering[k], mine_in)
        for k in range(count - 1, 0, -1):
            (_, resp_k), (_, start_k) = pair(a, k), pair(b, k)
            state = step * state + resp_k * entering[k] + start_k
            mine_after = jnp.where(me == k - 1, state, mine_after)
        return mine_in, mine_after

    sent = []
    base_z = n_span - 1
    base_y = base_z + n_z - 1
    late = base_y + n_y - 1
    len_z, len_y = n_span * frames, n_z * n_span * frames
    exchange(a1, span, span_peers, 0)

    def modal_part(j):
        cols = pl.ds(pl.multiple_of(((x + j) % n_x) * 2 * LANES, 2 * LANES), 2 * LANES)
        return jnp.dot(
            slopes_ref[:, cols], rbuf[j].reshape(2 * LANES, modes), preferred_element_type=F32
        )

    recon.relay_second()
    keep_r.wait()
    keep_s.wait()
    recon.wait_chip(0)
    modal[...] = modal_part(0)
    recon.relay_third()
    inter.begin_first()
    recon.wait_chip(3)
    modal[...] += modal_part(3)
    recon.wait_chip(1)
    modal[...] += modal_part(1)
    recon.wait_chip(2)
    modal[...] += modal_part(2)
    collect(a1, span, span_peers, 0)
    put(a2, z, total_a(a1, n_span, frames))
    exchange(a2, z, z_peers, base_z)

    for l in range(tiles):
        p1, p2, p4, pw, f8 = (cst[l, n] for n in range(5))
        inject = cst[l, 10]
        parts = []
        for k in range(blocks):
            v = inject * modal[pl.ds(k * ROWS, ROWS), lane(l)]
            v = v + p1 * pltpu.roll(v, 1, 0)
            v = v + p2 * pltpu.roll(v, 2, 0)
            v = v + p4 * pltpu.roll(v, 4, 0)
            parts.append(v)
        before = jnp.zeros((ROWS, LANES), F32)
        filtered = []
        for k in range(blocks):
            filtered.append(parts[k] + pw * before)
            before = f8 * before + jnp.broadcast_to(parts[k][ROWS - 1:], (ROWS, LANES))
        first = back_scan(lambda k: filtered[k], state0, l)
        b1[span, pl.ds(l, 1), :] = before[0:1]
        b1[span, pl.ds(tiles + l, 1), :] = first

    exchange(b1, span, span_peers, late)
    inter.begin_second()
    inter.relay_first()
    collect(b1, span, span_peers, late)
    put(b2, z, total_b(a1, b1, n_span, frames))
    exchange(b2, z, z_peers, late + base_z)
    collect(a2, z, z_peers, base_z)
    put(a3, y, total_a(a2, n_z, len_z))
    exchange(a3, y, y_peers, base_y)
    inter.relay_second()
    form_x = affine(a1, b1, span, n_span, frames)
    collect(b2, z, z_peers, late + base_z)
    put(b3, y, total_b(a2, b2, n_z, len_z))
    exchange(b3, y, y_peers, late + base_y)
    inter.relay_third()
    form_z = affine(a2, b2, z, n_z, len_z)
    collect(a3, y, y_peers, base_y)
    collect(b3, y, y_peers, late + base_y)

    before, after = solve_top(a3, b3, y, n_y, len_y)
    before, after = apply(form_z, before, after)
    before, after = apply(form_x, before, after)
    carry[pl.ds(0, tiles), :] = before
    carry[pl.ds(tiles, tiles), :] = after
    for l in range(tiles):
        state = (
            state0[:, lane(l)]
            + back_in[:, lane(l)] * carry[pl.ds(tiles + l, 1), :]
            + fwd_in[:, lane(l)] * carry[pl.ds(l, 1), :]
        )
        smooth_ref[:, lane(l)] = state.astype(jnp.bfloat16)

    keep_i.wait()
    for j in (0, 3, 1, 2):
        inter.wait_chip(j)
        cols = pl.ds(pl.multiple_of(((x + j) % n_x) * 2 * LANES, 2 * LANES), 2 * LANES)
        fitted = jnp.dot(smooth_ref[...], ibuf[j], preferred_element_type=F32)
        resid_ref[:, cols] = (slopes_ref[:, cols].astype(F32) - fitted).astype(jnp.bfloat16)

    recon.drain()
    inter.drain()
    for copy in sent:
        copy.wait_send()


def hand_over(smooth_in, resid_in, smooth_out, resid_out, sems):
    stores = (
        pltpu.make_async_copy(resid_in, resid_out, sems.at[0]),
        pltpu.make_async_copy(smooth_in, smooth_out, sems.at[1]),
    )
    for store in stores:
        store.start()
    for store in stores:
        store.wait()


def body(n_y, n_z, n_x, slopes, reconstructor, interaction, frame_valid, open_rate, closed_rate):
    frames, n_slopes = slopes.shape
    modes = reconstructor.shape[1]
    tiles = modes // LANES
    n_span = 2 * n_x
    messages = 2 * (n_span - 1 + n_z - 1 + n_y - 1)
    hbm = pl.BlockSpec(memory_space=pl.ANY)
    vmem = pl.BlockSpec(memory_space=pltpu.VMEM)
    far = pl.BlockSpec(memory_space=pltpu.HBM)
    whole = (frames, modes)
    pinned = [
        pltpu.with_memory_space_constraint(v, pltpu.HBM)
        for v in (
            slopes, reconstructor, interaction,
            open_rate.reshape(1, modes), closed_rate.reshape(1, modes),
        )
    ]
    smoothed, residual = pl.pallas_call(
        functools.partial(kernel, n_y, n_z, n_x),
        out_shape=(
            jax.ShapeDtypeStruct((frames, modes), jnp.bfloat16),
            jax.ShapeDtypeStruct((frames, n_slopes), jnp.bfloat16),
        ),
        in_specs=[far, far, far, vmem, far, far],
        out_specs=(vmem, vmem),
        scratch_shapes=[
            pltpu.VMEM((1, modes), F32),
            pltpu.VMEM((1, modes), F32),
            pltpu.VMEM((frames, n_slopes), jnp.bfloat16),
            pltpu.VMEM((n_x, 2, LANES, modes), jnp.bfloat16),
            pltpu.VMEM((n_x, modes, 2 * LANES), jnp.bfloat16),
            pltpu.VMEM(whole, F32),
            pltpu.VMEM(whole, F32),
            pltpu.VMEM(whole, F32),
            pltpu.VMEM(whole, F32),
            pltpu.VMEM((tiles, 12, ROWS, LANES), F32),
            pltpu.VMEM((2 * tiles, LANES), F32),
            pltpu.VMEM((2 * tiles, LANES), F32),
            *[pltpu.VMEM((n, 2 * tiles, LANES), F32) for n in (n_span, n_z, n_y) * 2],
            pltpu.SemaphoreType.DMA((5,)),
            pltpu.SemaphoreType.DMA((13,)),
            pltpu.SemaphoreType.DMA((13,)),
            pltpu.SemaphoreType.DMA((13,)),
            pltpu.SemaphoreType.DMA((13,)),
            pltpu.SemaphoreType.DMA((messages,)),
            pltpu.SemaphoreType.DMA((messages,)),
        ],
        compiler_params=pltpu.CompilerParams(
            collective_id=0, has_side_effects=True, vmem_limit_bytes=16 << 20
        ),
    )(
        *pinned[:3],
        frame_valid.reshape(1, 1),
        *pinned[3:],
    )
    return pl.pallas_call(
        hand_over,
        out_shape=(
            jax.ShapeDtypeStruct((frames, modes), jnp.bfloat16),
            jax.ShapeDtypeStruct((frames, n_slopes), jnp.bfloat16),
        ),
        in_specs=[hbm, hbm],
        out_specs=(far, far),
        scratch_shapes=[pltpu.SemaphoreType.DMA((2,))],
        compiler_params=pltpu.CompilerParams(vmem_limit_bytes=8 << 20),
    )(smoothed, residual)


def solution(mesh):
    grp, span = mesh.shape["grp"], mesh.shape["span"]
    n_z = 8 if grp % 8 == 0 else 1
    in_specs = (
        P(("grp", "span"), None),
        P("span", None),
        P(None, "span"),
        P(("grp", "span")),
        P(),
        P(),
    )
    out_specs = (P(("grp", "span"), None), P(("grp", "span"), None))
    return jax.shard_map(
        functools.partial(body, grp // n_z, n_z, span // 2),
        mesh=mesh, in_specs=in_specs, out_specs=out_specs, check_vma=False,
    )
```
